32 devices in a mesh: group: 2 (over y), patch: 4 (over z), head: 2 (over x), cfg: 2 (over core).
Axes of the slice: x: 2, y: 2, z: 4, core: 2. Of those that a mesh axis runs over, the one named last changes fastest.
Arguments:
- fresh_query: bfloat16 [4, 256, 2560], P(('group', 'cfg'), ('patch', 'head')), parts along dimension 0, may hold values from -32 to 32
- fresh_key: bfloat16 [4, 256, 2560], P(('group', 'cfg'), ('patch', 'head')), parts along dimension 0, may hold values from -9 to 9
- fresh_value: bfloat16 [4, 256, 2560], P(('group', 'cfg'), ('patch', 'head')), parts along dimension 0, may hold values from -12 to 12
- stale_key: bfloat16 [4, 256, 2560], P(('group', 'cfg'), 'patch', 'head'), parts along dimension 0, may hold values from -8 to 8
- stale_value: bfloat16 [4, 256, 2560], P(('group', 'cfg'), 'patch', 'head'), parts along dimension 0, may hold values from -12 to 12
- cross_query: bfloat16 [4, 256, 2560], P(('group', 'cfg'), ('patch', 'head')), parts along dimension 0, may hold values from -32 to 32
- text_key: bfloat16 [4, 512, 2560], P(('group', 'cfg'), None, 'head'), parts along dimension 0, may hold values from -8 to 8
- text_value: bfloat16 [4, 512, 2560], P(('group', 'cfg'), None, 'head'), parts along dimension 0, may hold values from -12 to 12
- text_mask: int32 [4, 512], P(('group', 'cfg')), parts along dimension 0, may hold values from 0 to 1, as said below
Outputs:
- self_mixed: bfloat16 [4, 256, 2560], P(('group', 'cfg'), ('patch', 'head')), parts along dimension 0
- cross_mixed: bfloat16 [4, 256, 2560], P(('group', 'cfg'), ('patch', 'head')), parts along dimension 0
The draws below stay inside these ranges and needn't reach their ends.
There are 2 independent parts, one for each index of `group`. The reference program is written for one: setup_inputs(seed, part) draws one part's arguments, and reference() takes and returns one part's arrays. A program takes and returns all parts, laid end to end along the dimension named above; each array names one. Nothing has to cross between parts.
Inputs may be any that keep to these rules, and one draw needn't show every extreme that they name: In each branch the ones of text_mask form a prefix of 32 or more positions; in one of the two branches all 512 are ones, in the other some are zeros.
All inputs are finite; a program needn't handle non-finite values.
Results may differ from the reference program's by a relative error of at most 0.005.
Values may be sent and summed in bfloat16 or wider, within the bound.
A program may use at most 128 MiB of HBM per device.

```python
import math
import jax
import jax.numpy as jnp
from jax import lax

HEADS = 20
HD = 128
TXT = 512
HW = 2560
PATCH_TOK = 64
TOKENS = 256
N_PATCH = 4


def keys_table(key, row_count):
    columns = HEADS * HD
    return 1.5 * jax.random.truncated_normal(key, -4.0, 4.0, (2, row_count, columns), jnp.float32)


def query_table(key, row_count):
    columns = HEADS * HD
    return 1.5 * jax.random.truncated_normal(key, -4.0, 4.0, (2, row_count, columns), jnp.float32)


def draw_stale_key(key, part):
    return keys_table(jax.random.fold_in(key, 11), TOKENS).astype(jnp.bfloat16)


def draw_text_key(key, part):
    return keys_table(jax.random.fold_in(key, 13), TXT).astype(jnp.bfloat16)


def draw_fresh_query(key, part):
    return query_table(jax.random.fold_in(key, 17), TOKENS).astype(jnp.bfloat16)


def draw_cross_query(key, part):
    return query_table(jax.random.fold_in(key, 19), TOKENS).astype(jnp.bfloat16)


def draw_text_mask(key, part):
    lowest = max(2, TXT // 16)
    partial_length = jax.random.randint(jax.random.fold_in(key, 31), (), lowest, TXT)
    full_branch = jax.random.randint(jax.random.fold_in(key, 37), (), 0, 2)
    lengths = jnp.where(jnp.arange(2) == full_branch, TXT, partial_length)
    return (jnp.arange(TXT)[None, :] < lengths[:, None]).astype(jnp.int32)


def steps_of(stream_key, dims, split, smallest, top_value):
    factor_of = 1.0
    for dim, shards_of in split:
        draws = jax.random.uniform(jax.random.fold_in(jax.random.fold_in(stream_key, 6), dim), (shards_of,), jnp.float32, smallest / len(split), top_value / len(split))
        factor_of = factor_of * jnp.repeat(jnp.exp(draws), dims[dim] // shards_of).reshape((-1,) + (1,) * (len(dims) - 1 - dim))
    return factor_of


def bell_draw(stream_key, dims, deviation, limit, split=(), kind=jnp.bfloat16):
    array = jax.random.normal(stream_key, dims, jnp.float32) * deviation
    if len(split) > 0:
        array = steps_of(stream_key, dims, split, -0.22, 0.18) * array
    return jnp.clip(array, min=-limit, max=limit).astype(kind)


def setup_inputs(seed: int = 0, part: int = 0) -> dict:
    keys = jax.random.split(jax.random.key(seed), 10)
    part_keys = jax.random.split(jax.random.fold_in(keys[9], part), 10)
    return {
        "fresh_query": draw_fresh_query(jax.random.fold_in(jax.random.fold_in(keys[9], part), 71), part),
        "fresh_key": bell_draw(part_keys[1], (2, TOKENS, HW), 1.5, 9.0, ((0, 2), (1, 8))),
        "fresh_value": bell_draw(part_keys[2], (2, TOKENS, HW), 2.0, 12.0, ((0, 2), (1, 8))),
        "stale_key": draw_stale_key(jax.random.fold_in(jax.random.fold_in(keys[9], part), 71), part),
        "stale_value": bell_draw(part_keys[4], (2, TOKENS, HW), 2.0, 12.0, ((0, 2), (1, 4), (2, 2))),
        "cross_query": draw_cross_query(jax.random.fold_in(jax.random.fold_in(keys[9], part), 71), part),
        "text_key": draw_text_key(jax.random.fold_in(jax.random.fold_in(keys[9], part), 71), part),
        "text_value": bell_draw(part_keys[7], (2, TXT, HW), 2.0, 12.0, ((0, 2), (2, 2))),
        "text_mask": draw_text_mask(jax.random.fold_in(jax.random.fold_in(keys[9], part), 71), part),
    }


def softmax_mix(queries, all_keys, all_values, usable):
    head_queries = queries.reshape(queries.shape[0], HEADS, HD).astype(jnp.float32)
    head_keys = all_keys.reshape(all_keys.shape[0], HEADS, HD).astype(jnp.float32)
    head_values = all_values.reshape(all_values.shape[0], HEADS, HD).astype(jnp.float32)
    scores = jnp.einsum('qhd,khd->qhk', head_queries, head_keys) * (1.0 / math.sqrt(HD))
    if usable is None:
        row_top = lax.optimization_barrier(jnp.max(scores, axis=-1, keepdims=True))
        weights = jnp.exp(scores - row_top)
    else:
        row_top = lax.optimization_barrier(jnp.max(jnp.where(usable, scores, -jnp.inf), axis=-1, keepdims=True))
        weights = jnp.where(usable, jnp.exp(jnp.where(usable, scores, row_top) - row_top), 0.0)
    totals = lax.optimization_barrier(jnp.sum(weights, axis=-1, keepdims=True))
    rounded = lax.optimization_barrier(weights.astype(jnp.bfloat16)).astype(jnp.float32)
    mixture = jnp.einsum('qhk,khd->qhd', rounded, head_values) / totals
    return mixture.reshape(queries.shape[0], HEADS * HD).astype(jnp.bfloat16)

def self_branch(queries, keys_new, values_new, keys_old, values_old):

    def one_patch(patch_index):
        offset = patch_index * PATCH_TOK
        all_keys = lax.dynamic_update_slice(keys_old, lax.dynamic_slice_in_dim(keys_new, offset, PATCH_TOK, 0), (offset, jnp.int32(0)))
        all_values = lax.dynamic_update_slice(values_old, lax.dynamic_slice_in_dim(values_new, offset, PATCH_TOK, 0), (offset, jnp.int32(0)))
        return softmax_mix(lax.dynamic_slice_in_dim(queries, offset, PATCH_TOK, 0), all_keys, all_values, None)
    blocks = lax.map(one_patch, jnp.arange(N_PATCH, dtype=jnp.int32))
    return blocks.reshape(TOKENS, HEADS * HD)

def cross_branch(queries, text_keys, text_values, mask_row):
    usable = (mask_row > 0)[None, None, :]

    def one_patch(patch_index):
        offset = patch_index * PATCH_TOK
        return softmax_mix(lax.dynamic_slice_in_dim(queries, offset, PATCH_TOK, 0), text_keys, text_values, usable)
    blocks = lax.map(one_patch, jnp.arange(N_PATCH, dtype=jnp.int32))
    return blocks.reshape(TOKENS, HEADS * HD)

def reference(fresh_query, fresh_key, fresh_value, stale_key, stale_value, cross_query, text_key, text_value, text_mask):
    self_parts = []
    cross_parts = []
    for branch in range(2):
        self_parts.append(self_branch(fresh_query[branch], fresh_key[branch], fresh_value[branch], stale_key[branch], stale_value[branch]))
        cross_parts.append(cross_branch(cross_query[branch], text_key[branch], text_value[branch], text_mask[branch]))
    return (jnp.stack(self_parts), jnp.stack(cross_parts))
```

```python
import functools
import math

import jax
import jax.numpy as jnp
from jax import lax
from jax.experimental import pallas as pl
from jax.experimental.pallas import tpu as pltpu
from jax.sharding import PartitionSpec as P

HD = 128
MESH = pl.DeviceIdType.MESH


def dot_nt(a, b):
    return lax.dot_general(a, b, (((1,), (1,)), ((), ())), preferred_element_type=jnp.float32)


def kernel(
    n_patch, n_head, nch,
    fq, fk, fv, sk, sv, cq, tk, tv, mask,
    so, co,
    fx, kv, txk, txv, mk, outs, outc,
    x_send, x_recv, x_loc, t_loc, kv_loc, own_send, fwd_send, kv_recv,
    o_send, o_recv, o_loc, c_send, c_recv, c_loc,
):
    p = lax.axis_index("patch")
    h = lax.axis_index("head")
    rows = fq.shape[1]
    prows = rows * n_head
    hcols = sk.shape[2]
    ccols = hcols // nch
    heads = hcols // HD
    cheads = heads // nch
    scale = 1.0 / math.sqrt(HD)
    fresh = (cq, fq, fk, fv)
    my_rows = pl.ds(pl.multiple_of(h * rows, rows), rows)

    for c in range(nch):
        for i, ref in enumerate((sk, sv)):
            pltpu.make_async_copy(
                ref.at[0, :, pl.ds(c * ccols, ccols)], kv.at[p, c, i], kv_loc.at[c, i]
            ).start()
    text_copies = [
        pltpu.make_async_copy(mask, mk, t_loc.at[0]),
        pltpu.make_async_copy(tk.at[0], txk, t_loc.at[1]),
        pltpu.make_async_copy(tv.at[0], txv, t_loc.at[2]),
    ]
    own_copies = [
        pltpu.make_async_copy(
            ref.at[0, :, pl.ds(pl.multiple_of(h * hcols, hcols), hcols)],
            fx.at[a, my_rows, :],
            x_loc.at[a],
        )
        for a, ref in enumerate(fresh)
    ]
    for cp in own_copies + text_copies:
        cp.start()

    barrier = pltpu.get_barrier_semaphore()
    has_right = p < n_patch - 1
    has_left = p > 0

    @pl.when(has_right)
    def _():
        pl.semaphore_signal(barrier, inc=1, device_id={"patch": p + 1}, device_id_type=MESH)

    @pl.when(has_left)
    def _():
        pl.semaphore_signal(barrier, inc=1, device_id={"patch": p - 1}, device_id_type=MESH)

    for k in range(1, n_head):
        pl.semaphore_signal(
            barrier, inc=1, device_id={"head": lax.rem(h + k, n_head)}, device_id_type=MESH
        )
    pl.semaphore_wait(
        barrier, n_head - 1 + has_right.astype(jnp.int32) + has_left.astype(jnp.int32)
    )

    def x_copy(a, k):
        peer = lax.rem(h + k, n_head)
        return pltpu.make_async_remote_copy(
            src_ref=fresh[a].at[0, :, pl.ds(pl.multiple_of(peer * hcols, hcols), hcols)],
            dst_ref=fx.at[a, my_rows, :],
            send_sem=x_send.at[a, k - 1],
            recv_sem=x_recv.at[a, k - 1],
            device_id={"head": peer},
            device_id_type=MESH,
        )

    def kv_copy(src, c, target, sem):
        return pltpu.make_async_remote_copy(
            src_ref=kv.at[src, c],
            dst_ref=kv.at[src, c],
            send_sem=sem,
            recv_sem=kv_recv.at[src, c],
            device_id={"patch": target},
            device_id_type=MESH,
        )

    for a in range(4):
        for k in range(1, n_head):
            x_copy(a, k).start()
    for c in range(nch):
        for i, ref in enumerate((sk, sv)):
            pltpu.make_async_copy(
                ref.at[0, :, pl.ds(c * ccols, ccols)], kv.at[p, c, i], kv_loc.at[c, i]
            ).wait()

        @pl.when(has_right)
        def _():
            kv_copy(p, c, p + 1, own_send.at[0, c]).start()

        @pl.when(has_left)
        def _():
            kv_copy(p, c, p - 1, own_send.at[1, c]).start()

    shorter = jnp.minimum(p, n_patch - 1 - p)

    def slot_source(s):
        near = s // 2 + 1
        near_src = jnp.where(s % 2 == 0, p - near, p + near)
        far = s - shorter + 1
        far_src = jnp.where(p > shorter, p - far, p + far)
        return jnp.where(s < 2 * shorter, near_src, far_src)

    def forward_target(src):
        target = jnp.where(src < p, p + 1, p - 1)
        return target, (target >= 0) & (target < n_patch)

    def forward(s, c):
        src = slot_source(s)
        kv_copy(src, c, p, fwd_send.at[s, c]).wait_recv()
        target, valid = forward_target(src)

        @pl.when(valid)
        def _():
            kv_copy(src, c, target, fwd_send.at[s, c]).start()

    def wait_x(a):
        own_copies[a].wait()
        for k in range(1, n_head):
            x_copy(a, k).wait_recv()

    def out_copy(src, dst, c, k, send, recv):
        peer = lax.rem(h + k, n_head)
        return pltpu.make_async_remote_copy(
            src_ref=src.at[c, pl.ds(pl.multiple_of(peer * rows, rows), rows), :],
            dst_ref=dst.at[0, :, pl.ds(pl.multiple_of(h * hcols + c * ccols, HD), ccols)],
            send_sem=send.at[c, k - 1],
            recv_sem=recv.at[c, k - 1],
            device_id={"head": peer},
            device_id_type=MESH,
        )

    def local_out(src, dst, c, sem):
        return pltpu.make_async_copy(
            src.at[c, my_rows, :],
            dst.at[0, :, pl.ds(pl.multiple_of(h * hcols + c * ccols, HD), ccols)],
            sem.at[c],
        )

    def send_out(src, dst, c, send, recv, loc):
        for k in range(1, n_head):
            out_copy(src, dst, c, k, send, recv).start()
        local_out(src, dst, c, loc).start()

    def cross_chunk(c):
        usable = mk[...] > 0
        for i in range(cheads):
            cols = pl.ds((c * cheads + i) * HD, HD)
            scores = dot_nt(fx[0, :, cols], txk[:, cols]) * scale
            scores = jnp.where(usable, scores, -jnp.inf)
            top = jnp.max(scores, axis=-1, keepdims=True)
            weights = jnp.exp(scores - top)
            total = jnp.sum(weights, axis=-1, keepdims=True)
            mix = jnp.dot(
                weights.astype(jnp.bfloat16), txv[:, cols], preferred_element_type=jnp.float32
            )
            outc[c, :, i * HD : (i + 1) * HD] = (mix / total).astype(jnp.bfloat16)

    def first(j):
        cols = pl.ds(j * HD, HD)
        scores = dot_nt(fx[1, :, cols], fx[2, :, cols]) * scale
        top = jnp.max(scores, axis=-1, keepdims=True)
        weights = jnp.exp(scores - top)
        total = jnp.sum(weights, axis=-1, keepdims=True)
        mix = jnp.dot(
            weights.astype(jnp.bfloat16), fx[3, :, cols], preferred_element_type=jnp.float32
        )
        return top, total, mix

    def absorb(state, src, j):
        top, total, mix = state
        c, i = divmod(j, cheads)
        cols = pl.ds(i * HD, HD)
        scores = dot_nt(fx[1, :, pl.ds(j * HD, HD)], kv[src, c, 0, :, cols]) * scale
        new_top = jnp.maximum(top, jnp.max(scores, axis=-1, keepdims=True))
        weights = jnp.exp(scores - new_top)
        factor = jnp.exp(top - new_top)
        total = total * factor + jnp.sum(weights, axis=-1, keepdims=True)
        mix = mix * factor + jnp.dot(
            weights.astype(jnp.bfloat16), kv[src, c, 1, :, cols],
            preferred_element_type=jnp.float32,
        )
        return new_top, total, mix

    half = (nch + 1) // 2
    for cp in text_copies:
        cp.wait()
    wait_x(0)
    for c in range(half):
        cross_chunk(c)
    for c in range(half):
        forward(0, c)
    for c in range(half, nch):
        cross_chunk(c)
    for c in range(nch):
        send_out(outc, co, c, c_send, c_recv, c_loc)
    for c in range(half, nch):
        forward(0, c)
    for a in range(1, 4):
        wait_x(a)
    states = [first(j) for j in range(heads)]
    src = slot_source(0)
    states = [absorb(states[j], src, j) for j in range(heads)]

    def slot(s, states):
        src = slot_source(s)
        out = []
        for c in range(nch):
            forward(s, c)
            for j in range(c * cheads, (c + 1) * cheads):
                out.append(absorb(states[j], src, j))
        return out

    if n_patch <= 8:
        for s in range(1, n_patch - 2):
            states = slot(s, states)
    else:
        states = lax.fori_loop(1, n_patch - 2, slot, states)
    last = n_patch - 2
    src = slot_source(last)
    for c in range(nch):
        if last > 0:
            forward(last, c)
        for i in range(cheads):
            j = c * cheads + i
            _, total, mix = absorb(states[j], src, j) if last > 0 else states[j]
            outs[c, :, i * HD : (i + 1) * HD] = (mix / total).astype(jnp.bfloat16)
        if c > 0:
            send_out(outs, so, c - 1, o_send, o_recv, o_loc)
    send_out(outs, so, nch - 1, o_send, o_recv, o_loc)

    for c in range(nch):

        @pl.when(has_right)
        def _():
            kv_copy(p, c, p + 1, own_send.at[0, c]).wait_send()

        @pl.when(has_left)
        def _():
            kv_copy(p, c, p - 1, own_send.at[1, c]).wait_send()

    def drain(s, carry):
        for c in range(nch):
            target, valid = forward_target(slot_source(s))

            @pl.when(valid)
            def _():
                kv_copy(slot_source(s), c, target, fwd_send.at[s, c]).wait_send()

        return carry

    if n_patch <= 8:
        for s in range(n_patch - 1):
            drain(s, 0)
    else:
        lax.fori_loop(0, n_patch - 1, drain, 0)
    for a in range(4):
        for k in range(1, n_head):
            x_copy(a, k).wait_send()
    for src_ref, dst, send, recv, loc in (
        (outc, co, c_send, c_recv, c_loc),
        (outs, so, o_send, o_recv, o_loc),
    ):
        for c in range(nch):
            for k in range(1, n_head):
                cp = out_copy(src_ref, dst, c, k, send, recv)
                cp.wait_send()
                cp.wait_recv()
            local_out(src_ref, dst, c, loc).wait()


def per_device(n_patch, n_head, *args):
    fq, fk, fv, sk, sv, cq, tk, tv, mask = args
    rows = fq.shape[1]
    prows = rows * n_head
    hcols = sk.shape[2]
    heads = hcols // HD
    nch = 5 if heads % 5 == 0 else 1
    ccols = hcols // nch
    txt = tk.shape[1]
    peers = max(n_head - 1, 1)
    any_spec = pl.BlockSpec(memory_space=pl.ANY)
    dma = pltpu.SemaphoreType.DMA
    bf16 = jnp.bfloat16
    return pl.pallas_call(
        functools.partial(kernel, n_patch, n_head, nch),
        out_shape=(
            jax.ShapeDtypeStruct(fq.shape, bf16),
            jax.ShapeDtypeStruct(cq.shape, bf16),
        ),
        in_specs=[any_spec] * 9,
        out_specs=(any_spec, any_spec),
        scratch_shapes=[
            pltpu.VMEM((4, prows, hcols), bf16),
            pltpu.VMEM((n_patch, nch, 2, prows, ccols), bf16),
            pltpu.VMEM((txt, hcols), bf16),
            pltpu.VMEM((txt, hcols), bf16),
            pltpu.VMEM((1, txt), jnp.int32),
            pltpu.VMEM((nch, prows, ccols), bf16),
            pltpu.VMEM((nch, prows, ccols), bf16),
            dma((4, peers)),
            dma((4, peers)),
            dma((4,)),
            dma((3,)),
            dma((nch, 2)),
            dma((2, nch)),
            dma((n_patch, nch)),
            dma((n_patch, nch)),
            dma((nch, peers)),
            dma((nch, peers)),
            dma((nch,)),
            dma((nch, peers)),
            dma((nch, peers)),
            dma((nch,)),
        ],
        compiler_params=pltpu.CompilerParams(collective_id=0, has_side_effects=True),
        name="displaced_attention",
    )(*args)


def solution(mesh):
    return jax.shard_map(
        functools.partial(per_device, mesh.shape["patch"], mesh.shape["head"]),
        mesh=mesh,
        in_specs=(
            P(("group", "cfg"), ("patch", "head"), None),
            P(("group", "cfg"), ("patch", "head"), None),
            P(("group", "cfg"), ("patch", "head"), None),
            P(("group", "cfg"), "patch", "head"),
            P(("group", "cfg"), "patch", "head"),
            P(("group", "cfg"), ("patch", "head"), None),
            P(("group", "cfg"), None, "head"),
            P(("group", "cfg"), None, "head"),
            P(("group", "cfg"), None),
        ),
        out_specs=(
            P(("group", "cfg"), ("patch", "head"), None),
            P(("group", "cfg"), ("patch", "head"), None),
        ),
        check_vma=False,
    )
```

```python
import functools
import math

import jax
import jax.numpy as jnp
from jax import lax
from jax.experimental import pallas as pl
from jax.experimental.pallas import tpu as pltpu
from jax.sharding import PartitionSpec as P

HD = 128
MESH = pl.DeviceIdType.MESH


def dot_nt(a, b):
    return lax.dot_general(a, b, (((1,), (1,)), ((), ())), preferred_element_type=jnp.float32)


def kernel(
    n_patch, n_head, nch,
    fq, fk, fv, sk, sv, cq, tk, tv, mask,
    so, co,
    fx, kv, txk, txv, mk, outs, outc,
    x_send, x_recv, x_loc, t_loc, kv_loc, own_send, fwd_send, kv_recv,
    o_send, o_recv, o_loc, c_send, c_recv, c_loc,
):
    p = lax.axis_index("patch")
    h = lax.axis_index("head")
    rows = fq.shape[1]
    prows = rows * n_head
    hcols = sk.shape[2]
    ccols = hcols // nch
    heads = hcols // HD
    cheads = heads // nch
    scale = 1.0 / math.sqrt(HD)
    fresh = (cq, fq, fk, fv)
    my_rows = pl.ds(pl.multiple_of(h * rows, rows), rows)

    for c in range(nch):
        for i, ref in enumerate((sk, sv)):
            pltpu.make_async_copy(
                ref.at[0, :, pl.ds(c * ccols, ccols)], kv.at[p, c, i], kv_loc.at[c, i]
            ).start()
    text_copies = [
        pltpu.make_async_copy(mask, mk, t_loc.at[0]),
        pltpu.make_async_copy(tk.at[0], txk, t_loc.at[1]),
        pltpu.make_async_copy(tv.at[0], txv, t_loc.at[2]),
    ]
    own_copies = [
        pltpu.make_async_copy(
            ref.at[0, :, pl.ds(pl.multiple_of(h * hcols, hcols), hcols)],
            fx.at[a, my_rows, :],
            x_loc.at[a],
        )
        for a, ref in enumerate(fresh)
    ]
    for cp in own_copies + text_copies:
        cp.start()

    barrier = pltpu.get_barrier_semaphore()
    has_right = p < n_patch - 1
    has_left = p > 0

    @pl.when(has_right)
    def _():
        pl.semaphore_signal(barrier, inc=1, device_id={"patch": p + 1}, device_id_type=MESH)

    @pl.when(has_left)
    def _():
        pl.semaphore_signal(barrier, inc=1, device_id={"patch": p - 1}, device_id_type=MESH)

    for k in range(1, n_head):
        pl.semaphore_signal(
            barrier, inc=1, device_id={"head": lax.rem(h + k, n_head)}, device_id_type=MESH
        )
    pl.semaphore_wait(
        barrier, n_head - 1 + has_right.astype(jnp.int32) + has_left.astype(jnp.int32)
    )

    def x_copy(a, k):
        peer = lax.rem(h + k, n_head)
        return pltpu.make_async_remote_copy(
            src_ref=fresh[a].at[0, :, pl.ds(pl.multiple_of(peer * hcols, hcols), hcols)],
            dst_ref=fx.at[a, my_rows, :],
            send_sem=x_send.at[a, k - 1],
            recv_sem=x_recv.at[a, k - 1],
            device_id={"head": peer},
            device_id_type=MESH,
        )

    def kv_copy(src, c, target, sem):
        return pltpu.make_async_remote_copy(
            src_ref=kv.at[src, c],
            dst_ref=kv.at[src, c],
            send_sem=sem,
            recv_sem=kv_recv.at[src, c],
            device_id={"patch": target},
            device_id_type=MESH,
        )

    for a in range(4):
        for k in range(1, n_head):
            x_copy(a, k).start()
    for c in range(nch):
        for i, ref in enumerate((sk, sv)):
            pltpu.make_async_copy(
                ref.at[0, :, pl.ds(c * ccols, ccols)], kv.at[p, c, i], kv_loc.at[c, i]
            ).wait()

        @pl.when(has_right)
        def _():
            kv_copy(p, c, p + 1, own_send.at[0, c]).start()

        @pl.when(has_left)
        def _():
            kv_copy(p, c, p - 1, own_send.at[1, c]).start()

    shorter = jnp.minimum(p, n_patch - 1 - p)

    def slot_source(s):
        near = s // 2 + 1
        near_src = jnp.where(s % 2 == 0, p - near, p + near)
        far = s - shorter + 1
        far_src = jnp.where(p > shorter, p - far, p + far)
        return jnp.where(s < 2 * shorter, near_src, far_src)

    def forward_target(src):
        target = jnp.where(src < p, p + 1, p - 1)
        return target, (target >= 0) & (target < n_patch)

    def forward(s, c):
        src = slot_source(s)
        kv_copy(src, c, p, fwd_send.at[s, c]).wait_recv()
        target, valid = forward_target(src)

        @pl.when(valid)
        def _():
            kv_copy(src, c, target, fwd_send.at[s, c]).start()

    def wait_x(a):
        own_copies[a].wait()
        for k in range(1, n_head):
            x_copy(a, k).wait_recv()

    def out_copy(src, dst, c, k, send, recv):
        peer = lax.rem(h + k, n_head)
        return pltpu.make_async_remote_copy(
            src_ref=src.at[c, pl.ds(pl.multiple_of(peer * rows, rows), rows), :],
            dst_ref=dst.at[0, :, pl.ds(pl.multiple_of(h * hcols + c * ccols, HD), ccols)],
            send_sem=send.at[c, k - 1],
            recv_sem=recv.at[c, k - 1],
            device_id={"head": peer},
            device_id_type=MESH,
        )

    def local_out(src, dst, c, sem):
        return pltpu.make_async_copy(
            src.at[c, my_rows, :],
            dst.at[0, :, pl.ds(pl.multiple_of(h * hcols + c * ccols, HD), ccols)],
            sem.at[c],
        )

    def send_out(src, dst, c, send, recv, loc):
        for k in range(1, n_head):
            out_copy(src, dst, c, k, send, recv).start()
        local_out(src, dst, c, loc).start()

    def cross_chunk(c):
        usable = mk[...] > 0
        for i in range(cheads):
            cols = pl.ds((c * cheads + i) * HD, HD)
            scores = dot_nt(fx[0, :, cols], txk[:, cols]) * scale
            scores = jnp.where(usable, scores, -jnp.inf)
            top = jnp.max(scores, axis=-1, keepdims=True)
            weights = jnp.exp(scores - top)
            total = jnp.sum(weights, axis=-1, keepdims=True)
            mix = jnp.dot(
                weights.astype(jnp.bfloat16), txv[:, cols], preferred_element_type=jnp.float32
            )
            outc[c, :, i * HD : (i + 1) * HD] = (mix / total).astype(jnp.bfloat16)

    def first(j):
        cols = pl.ds(j * HD, HD)
        scores = dot_nt(fx[1, :, cols], fx[2, :, cols]) * scale
        top = jnp.max(scores, axis=-1, keepdims=True)
        weights = jnp.exp(scores - top)
        total = jnp.sum(weights, axis=-1, keepdims=True)
        mix = jnp.dot(
            weights.astype(jnp.bfloat16), fx[3, :, cols], preferred_element_type=jnp.float32
        )
        return top, total, mix

    def absorb(state, src, j):
        top, total, mix = state
        c, i = divmod(j, cheads)
        cols = pl.ds(i * HD, HD)
        scores = dot_nt(fx[1, :, pl.ds(j * HD, HD)], kv[src, c, 0, :, cols]) * scale
        new_top = jnp.maximum(top, jnp.max(scores, axis=-1, keepdims=True))
        weights = jnp.exp(scores - new_top)
        factor = jnp.exp(top - new_top)
        total = total * factor + jnp.sum(weights, axis=-1, keepdims=True)
        mix = mix * factor + jnp.dot(
            weights.astype(jnp.bfloat16), kv[src, c, 1, :, cols],
            preferred_element_type=jnp.float32,
        )
        return new_top, total, mix

    half = (nch + 1) // 2
    for cp in text_copies:
        cp.wait()
    wait_x(0)
    for c in range(half):
        cross_chunk(c)
    for c in range(half):
        forward(0, c)
    for c in range(half, nch):
        cross_chunk(c)
    for c in range(nch):
        send_out(outc, co, c, c_send, c_recv, c_loc)
    for c in range(half, nch):
        forward(0, c)
    for a in range(1, 4):
        wait_x(a)
    states = [first(j) for j in range(heads)]
    src = slot_source(0)
    states = [absorb(states[j], src, j) for j in range(heads)]

    def slot(s, states):
        src = slot_source(s)
        out = []
        for c in range(nch):
            forward(s, c)
            for j in range(c * cheads, (c + 1) * cheads):
                out.append(absorb(states[j], src, j))
        return out

    if n_patch <= 8:
        for s in range(1, n_patch - 2):
            states = slot(s, states)
    else:
        states = lax.fori_loop(1, n_patch - 2, slot, states)
    last = n_patch - 2
    src = slot_source(last)
    for c in range(nch):
        if last > 0:
            forward(last, c)
        for i in range(cheads):
            j = c * cheads + i
            _, total, mix = absorb(states[j], src, j) if last > 0 else states[j]
            outs[c, :, i * HD : (i + 1) * HD] = (mix / total).astype(jnp.bfloat16)
        if c > 0:
            send_out(outs, so, c - 1, o_send, o_recv, o_loc)
    send_out(outs, so, nch - 1, o_send, o_recv, o_loc)

    for c in range(nch):

        @pl.when(has_right)
        def _():
            kv_copy(p, c, p + 1, own_send.at[0, c]).wait_send()

        @pl.when(has_left)
        def _():
            kv_copy(p, c, p - 1, own_send.at[1, c]).wait_send()

    def drain(s, carry):
        for c in range(nch):
            target, valid = forward_target(slot_source(s))

            @pl.when(valid)
            def _():
                kv_copy(slot_source(s), c, target, fwd_send.at[s, c]).wait_send()

        return carry

    if n_patch <= 8:
        for s in range(n_patch - 1):
            drain(s, 0)
    else:
        lax.fori_loop(0, n_patch - 1, drain, 0)
    for a in range(4):
        for k in range(1, n_head):
            x_copy(a, k).wait_send()
    for src_ref, dst, send, recv, loc in (
        (outc, co, c_send, c_recv, c_loc),
        (outs, so, o_send, o_recv, o_loc),
    ):
        for c in range(nch):
            for k in range(1, n_head):
                cp = out_copy(src_ref, dst, c, k, send, recv)
                cp.wait_send()
                cp.wait_recv()
            local_out(src_ref, dst, c, loc).wait()


def store_kernel(a, b, so, co, sem):
    copies = [
        pltpu.make_async_copy(a, so, sem.at[0]),
        pltpu.make_async_copy(b, co, sem.at[1]),
    ]
    for cp in copies:
        cp.start()
    for cp in copies:
        cp.wait()


def store(a, b):
    return pl.pallas_call(
        store_kernel,
        out_shape=(
            jax.ShapeDtypeStruct(a.shape, a.dtype),
            jax.ShapeDtypeStruct(b.shape, b.dtype),
        ),
        in_specs=[pl.BlockSpec(memory_space=pltpu.VMEM)] * 2,
        out_specs=(pl.BlockSpec(memory_space=pltpu.HBM),) * 2,
        scratch_shapes=[pltpu.SemaphoreType.DMA((2,))],
        compiler_params=pltpu.CompilerParams(vmem_limit_bytes=1024 * 1024),
        name="store_outputs",
    )(a, b)


def per_device(n_patch, n_head, *args):
    fq, fk, fv, sk, sv, cq, tk, tv, mask = args
    rows = fq.shape[1]
    prows = rows * n_head
    hcols = sk.shape[2]
    heads = hcols // HD
    nch = 5 if heads % 5 == 0 else 1
    ccols = hcols // nch
    txt = tk.shape[1]
    peers = max(n_head - 1, 1)
    any_spec = pl.BlockSpec(memory_space=pl.ANY)
    dma = pltpu.SemaphoreType.DMA
    bf16 = jnp.bfloat16
    mixed = pl.pallas_call(
        functools.partial(kernel, n_patch, n_head, nch),
        out_shape=(
            pltpu.VMEM(fq.shape, bf16),
            pltpu.VMEM(cq.shape, bf16),
        ),
        in_specs=[any_spec] * 9,
        out_specs=(pl.BlockSpec(memory_space=pltpu.VMEM),) * 2,
        scratch_shapes=[
            pltpu.VMEM((4, prows, hcols), bf16),
            pltpu.VMEM((n_patch, nch, 2, prows, ccols), bf16),
            pltpu.VMEM((txt, hcols), bf16),
            pltpu.VMEM((txt, hcols), bf16),
            pltpu.VMEM((1, txt), jnp.int32),
            pltpu.VMEM((nch, prows, ccols), bf16),
            pltpu.VMEM((nch, prows, ccols), bf16),
            dma((4, peers)),
            dma((4, peers)),
            dma((4,)),
            dma((3,)),
            dma((nch, 2)),
            dma((2, nch)),
            dma((n_patch, nch)),
            dma((n_patch, nch)),
            dma((nch, peers)),
            dma((nch, peers)),
            dma((nch,)),
            dma((nch, peers)),
            dma((nch, peers)),
            dma((nch,)),
        ],
        compiler_params=pltpu.CompilerParams(collective_id=0, has_side_effects=True),
        name="displaced_attention",
    )(*args)
    return store(*mixed)


def solution(mesh):
    return jax.shard_map(
        functools.partial(per_device, mesh.shape["patch"], mesh.shape["head"]),
        mesh=mesh,
        in_specs=(
            P(("group", "cfg"), ("patch", "head"), None),
            P(("group", "cfg"), ("patch", "head"), None),
            P(("group", "cfg"), ("patch", "head"), None),
            P(("group", "cfg"), "patch", "head"),
            P(("group", "cfg"), "patch", "head"),
            P(("group", "cfg"), ("patch", "head"), None),
            P(("group", "cfg"), None, "head"),
            P(("group", "cfg"), None, "head"),
            P(("group", "cfg"), None),
        ),
        out_specs=(
            P(("group", "cfg"), ("patch", "head"), None),
            P(("group", "cfg"), ("patch", "head"), None),
        ),
        check_vma=False,
    )
```

```python
import functools
import math

import jax
import jax.numpy as jnp
from jax import lax
from jax.experimental import pallas as pl
from jax.experimental.pallas import tpu as pltpu
from jax.sharding import PartitionSpec as P

HD = 128
MESH = pl.DeviceIdType.MESH


def dot_nt(a, b):
    return lax.dot_general(a, b, (((1,), (1,)), ((), ())), preferred_element_type=jnp.float32)


def kernel(
    n_patch, n_head, nch,
    fq, fk, fv, sk, sv, cq, tk, tv, mask,
    so, co,
    fx, kv, txk, txv, mk, outs, outc,
    x_send, x_recv, x_loc, t_loc, kv_loc, own_send, fwd_send, kv_recv,
    o_send, o_recv, o_loc, c_send, c_recv, c_loc,
    dq, part_out, part_in, stat_out, stat_in, dq_sem, part_send, part_recv,
):
    p = lax.axis_index("patch")
    h = lax.axis_index("head")
    rows = fq.shape[1]
    prows = rows * n_head
    hcols = sk.shape[2]
    ccols = hcols // nch
    heads = hcols // HD
    cheads = heads // nch
    scale = 1.0 / math.sqrt(HD)
    fresh = (cq, fq, fk, fv)
    my_rows = pl.ds(pl.multiple_of(h * rows, rows), rows)

    for c in range(nch):
        for i, ref in enumerate((sk, sv)):
            pltpu.make_async_copy(
                ref.at[0, :, pl.ds(c * ccols, ccols)], kv.at[p, c, i], kv_loc.at[c, i]
            ).start()
    text_copies = [
        pltpu.make_async_copy(mask, mk, t_loc.at[0]),
        pltpu.make_async_copy(tk.at[0], txk, t_loc.at[1]),
        pltpu.make_async_copy(tv.at[0], txv, t_loc.at[2]),
    ]
    own_copies = [
        pltpu.make_async_copy(
            ref.at[0, :, pl.ds(pl.multiple_of(h * hcols, hcols), hcols)],
            fx.at[a, my_rows, :],
            x_loc.at[a],
        )
        for a, ref in enumerate(fresh)
    ]
    for cp in own_copies + text_copies:
        cp.start()

    barrier = pltpu.get_barrier_semaphore()
    has_right = p < n_patch - 1
    has_left = p > 0

    @pl.when(has_right)
    def _():
        pl.semaphore_signal(barrier, inc=1, device_id={"patch": p + 1}, device_id_type=MESH)

    @pl.when(has_left)
    def _():
        pl.semaphore_signal(barrier, inc=1, device_id={"patch": p - 1}, device_id_type=MESH)

    for k in range(1, n_head):
        pl.semaphore_signal(
            barrier, inc=1, device_id={"head": lax.rem(h + k, n_head)}, device_id_type=MESH
        )
    pl.semaphore_wait(
        barrier, n_head - 1 + has_right.astype(jnp.int32) + has_left.astype(jnp.int32)
    )

    def x_copy(a, k):
        peer = lax.rem(h + k, n_head)
        return pltpu.make_async_remote_copy(
            src_ref=fresh[a].at[0, :, pl.ds(pl.multiple_of(peer * hcols, hcols), hcols)],
            dst_ref=fx.at[a, my_rows, :],
            send_sem=x_send.at[a, k - 1],
            recv_sem=x_recv.at[a, k - 1],
            device_id={"head": peer},
            device_id_type=MESH,
        )

    def kv_copy(src, c, target, sem):
        return pltpu.make_async_remote_copy(
            src_ref=kv.at[src, c],
            dst_ref=kv.at[src, c],
            send_sem=sem,
            recv_sem=kv_recv.at[src, c],
            device_id={"patch": target},
            device_id_type=MESH,
        )

    for a in (1, 0, 2, 3):
        for k in range(1, n_head):
            x_copy(a, k).start()

    def wait_own_kv(c):
        for i, ref in enumerate((sk, sv)):
            pltpu.make_async_copy(
                ref.at[0, :, pl.ds(c * ccols, ccols)], kv.at[p, c, i], kv_loc.at[c, i]
            ).wait()

    def wait_x(a):
        own_copies[a].wait()
        for k in range(1, n_head):
            x_copy(a, k).wait_recv()

    def out_copy(src, dst, c, k, send, recv):
        peer = lax.rem(h + k, n_head)
        return pltpu.make_async_remote_copy(
            src_ref=src.at[c, pl.ds(pl.multiple_of(peer * rows, rows), rows), :],
            dst_ref=dst.at[0, :, pl.ds(pl.multiple_of(h * hcols + c * ccols, HD), ccols)],
            send_sem=send.at[c, k - 1],
            recv_sem=recv.at[c, k - 1],
            device_id={"head": peer},
            device_id_type=MESH,
        )

    def local_out(src, dst, c, sem):
        return pltpu.make_async_copy(
            src.at[c, my_rows, :],
            dst.at[0, :, pl.ds(pl.multiple_of(h * hcols + c * ccols, HD), ccols)],
            sem.at[c],
        )

    def send_out(src, dst, c, send, recv, loc):
        for k in range(1, n_head):
            out_copy(src, dst, c, k, send, recv).start()
        local_out(src, dst, c, loc).start()

    def cross_chunk(c):
        usable = mk[...] > 0
        for i in range(cheads):
            cols = pl.ds((c * cheads + i) * HD, HD)
            scores = dot_nt(fx[0, :, cols], txk[:, cols]) * scale
            scores = jnp.where(usable, scores, -jnp.inf)
            top = jnp.max(scores, axis=-1, keepdims=True)
            weights = jnp.exp(scores - top)
            total = jnp.sum(weights, axis=-1, keepdims=True)
            mix = jnp.dot(
                weights.astype(jnp.bfloat16), txv[:, cols], preferred_element_type=jnp.float32
            )
            outc[c, :, i * HD : (i + 1) * HD] = (mix / total).astype(jnp.bfloat16)

    def first(j):
        cols = pl.ds(j * HD, HD)
        return start(fx[1, :, cols], fx[2, :, cols], fx[3, :, cols])

    def start(q, keys, values):
        scores = dot_nt(q, keys) * scale
        top = jnp.max(scores, axis=-1, keepdims=True)
        weights = jnp.exp(scores - top)
        total = jnp.sum(weights, axis=-1, keepdims=True)
        mix = jnp.dot(
            weights.astype(jnp.bfloat16), values, preferred_element_type=jnp.float32
        )
        return top, total, mix

    def query(j):
        return fx[1, :, pl.ds(j * HD, HD)]

    def absorb(state, src, j, q=None):
        top, total, mix = state
        c, i = divmod(j, cheads)
        cols = pl.ds(i * HD, HD)
        q = query(j) if q is None else q
        scores = dot_nt(q, kv[src, c, 0, :, cols]) * scale
        new_top = jnp.maximum(top, jnp.max(scores, axis=-1, keepdims=True))
        weights = jnp.exp(scores - new_top)
        factor = jnp.exp(top - new_top)
        total = total * factor + jnp.sum(weights, axis=-1, keepdims=True)
        mix = mix * factor + jnp.dot(
            weights.astype(jnp.bfloat16), kv[src, c, 1, :, cols],
            preferred_element_type=jnp.float32,
        )
        return new_top, total, mix

    def line_program():
        for c in range(nch):
            wait_own_kv(c)

            @pl.when(has_right)
            def _():
                kv_copy(p, c, p + 1, own_send.at[0, c]).start()

            @pl.when(has_left)
            def _():
                kv_copy(p, c, p - 1, own_send.at[1, c]).start()

        shorter = jnp.minimum(p, n_patch - 1 - p)

        def slot_source(s):
            near = s // 2 + 1
            near_src = jnp.where(s % 2 == 0, p - near, p + near)
            far = s - shorter + 1
            far_src = jnp.where(p > shorter, p - far, p + far)
            return jnp.where(s < 2 * shorter, near_src, far_src)

        def forward_target(src):
            target = jnp.where(src < p, p + 1, p - 1)
            return target, (target >= 0) & (target < n_patch)

        def forward(s, c):
            src = slot_source(s)
            kv_copy(src, c, p, fwd_send.at[s, c]).wait_recv()
            target, valid = forward_target(src)

            @pl.when(valid)
            def _():
                kv_copy(src, c, target, fwd_send.at[s, c]).start()

        half = (nch + 1) // 2
        for cp in text_copies:
            cp.wait()
        wait_x(0)
        for c in range(half):
            cross_chunk(c)
        for c in range(half):
            forward(0, c)
        for c in range(half, nch):
            cross_chunk(c)
        for c in range(nch):
            send_out(outc, co, c, c_send, c_recv, c_loc)
        for c in range(half, nch):
            forward(0, c)
        for a in range(1, 4):
            wait_x(a)
        states = [first(j) for j in range(heads)]
        src = slot_source(0)
        states = [absorb(states[j], src, j) for j in range(heads)]

        def slot(s, states):
            src = slot_source(s)
            out = []
            for c in range(nch):
                forward(s, c)
                for j in range(c * cheads, (c + 1) * cheads):
                    out.append(absorb(states[j], src, j))
            return out

        if n_patch <= 8:
            for s in range(1, n_patch - 2):
                states = slot(s, states)
        else:
            states = lax.fori_loop(1, n_patch - 2, slot, states)
        last = n_patch - 2
        src = slot_source(last)
        for c in range(nch):
            if last > 0:
                forward(last, c)
            for i in range(cheads):
                j = c * cheads + i
                _, total, mix = absorb(states[j], src, j) if last > 0 else states[j]
                outs[c, :, i * HD : (i + 1) * HD] = (mix / total).astype(jnp.bfloat16)
            if c > 0:
                send_out(outs, so, c - 1, o_send, o_recv, o_loc)
        send_out(outs, so, nch - 1, o_send, o_recv, o_loc)

        for c in range(nch):

            @pl.when(has_right)
            def _():
                kv_copy(p, c, p + 1, own_send.at[0, c]).wait_send()

            @pl.when(has_left)
            def _():
                kv_copy(p, c, p - 1, own_send.at[1, c]).wait_send()

        def drain(s, carry):
            for c in range(nch):
                target, valid = forward_target(slot_source(s))

                @pl.when(valid)
                def _():
                    kv_copy(slot_source(s), c, target, fwd_send.at[s, c]).wait_send()

            return carry

        if n_patch <= 8:
            for s in range(n_patch - 1):
                drain(s, 0)
        else:
            lax.fori_loop(0, n_patch - 1, drain, 0)

    is_end = jnp.logical_not(has_right & has_left)
    across = n_patch - 1 - p
    lanes = lax.broadcasted_iota(jnp.int32, (prows, HD), 1)

    def neighbour(c, other):
        return [
            pltpu.make_async_remote_copy(
                src_ref=src.at[c],
                dst_ref=dst.at[c],
                send_sem=part_send.at[c, i],
                recv_sem=part_recv.at[c, i],
                device_id={"patch": other},
                device_id_type=MESH,
            )
            for i, (src, dst) in enumerate(((part_out, part_in), (stat_out, stat_in)))
        ]

    def dq_copy(other):
        return pltpu.make_async_remote_copy(
            src_ref=fx.at[1],
            dst_ref=dq,
            send_sem=dq_sem.at[0],
            recv_sem=dq_sem.at[1],
            device_id={"patch": other},
            device_id_type=MESH,
        )

    def end_program():
        helper = jnp.where(has_right, p + 1, p - 1)
        lead = min(2, nch)
        for c in range(lead):
            wait_own_kv(c)
            kv_copy(p, c, helper, own_send.at[0, c]).start()
        wait_x(1)
        dq_copy(helper).start()
        for c in range(lead, nch):
            wait_own_kv(c)
            kv_copy(p, c, helper, own_send.at[0, c]).start()
        for cp in text_copies:
            cp.wait()
        wait_x(0)
        for c in range(nch):
            cross_chunk(c)
            if c > 0:
                send_out(outc, co, c - 1, c_send, c_recv, c_loc)
        send_out(outc, co, nch - 1, c_send, c_recv, c_loc)
        wait_x(2)
        wait_x(3)
        states = [first(j) for j in range(heads)]
        for c in range(nch):
            for cp in neighbour(c, helper):
                cp.wait_recv()
            for i in range(cheads):
                top, total, mix = states[c * cheads + i]
                cols = slice(i * HD, (i + 1) * HD)
                lse = stat_in[c, :, i : i + 1]
                new_top = jnp.maximum(top, lse)
                mine = jnp.exp(top - new_top)
                theirs = jnp.exp(lse - new_top)
                mix = mix * mine + part_in[c, :, cols].astype(jnp.float32) * theirs
                outs[c, :, cols] = (mix / (total * mine + theirs)).astype(jnp.bfloat16)
            send_out(outs, so, c, o_send, o_recv, o_loc)
        for c in range(nch):
            kv_copy(p, c, helper, own_send.at[0, c]).wait_send()
        dq_copy(helper).wait_send()

    def helper_program():
        end = jnp.where(p < across, p - 1, p + 1)
        far = n_patch - 1 - end
        for c in range(nch):
            wait_own_kv(c)
            kv_copy(p, c, across, own_send.at[0, c]).start()

        def pass_on(c):
            kv_copy(end, c, across, fwd_send.at[0, c]).wait_recv()
            kv_copy(end, c, across, fwd_send.at[0, c]).start()

        pass_on(0)
        for cp in text_copies:
            cp.wait()
        wait_x(0)
        for c in range(nch):
            cross_chunk(c)
            if c > 0:
                send_out(outc, co, c - 1, c_send, c_recv, c_loc)
            if c + 1 < nch:
                pass_on(c + 1)
        send_out(outc, co, nch - 1, c_send, c_recv, c_loc)
        for a in range(1, 4):
            wait_x(a)
        dq_copy(end).wait_recv()

        def both(j):
            return jnp.concatenate([query(j), dq[:, pl.ds(j * HD, HD)]], axis=0)

        states = []
        for j in range(heads):
            c, i = divmod(j, cheads)
            cols = pl.ds(i * HD, HD)
            mine = absorb(first(j), end, j)
            theirs = start(
                dq[:, pl.ds(j * HD, HD)], kv[p, c, 0, :, cols], kv[p, c, 1, :, cols]
            )
            states.append([jnp.concatenate(pair, axis=0) for pair in zip(mine, theirs)])
        for c in range(nch):
            kv_copy(across, c, p, own_send.at[0, c]).wait_recv()
            for j in range(c * cheads, (c + 1) * cheads):
                states[j] = absorb(states[j], across, j, both(j))
        for c in range(nch):
            kv_copy(far, c, p, own_send.at[0, c]).wait_recv()
            stat = jnp.zeros((prows, HD), jnp.float32)
            for i in range(cheads):
                j = c * cheads + i
                top, total, mix = absorb(states[j], far, j, both(j))
                mixed = (mix / total).astype(jnp.bfloat16)
                lse = top[prows:] + jnp.log(total[prows:])
                stat = jnp.where(lanes == i, lse, stat)
                part_out[c, :, i * HD : (i + 1) * HD] = mixed[prows:]
                outs[c, :, i * HD : (i + 1) * HD] = mixed[:prows]
            stat_out[c] = stat
            for cp in neighbour(c, end):
                cp.start()
            send_out(outs, so, c, o_send, o_recv, o_loc)
        for c in range(nch):
            kv_copy(p, c, across, own_send.at[0, c]).wait_send()
            kv_copy(end, c, across, fwd_send.at[0, c]).wait_send()
            for cp in neighbour(c, end):
                cp.wait_send()

    if n_patch == 4:
        pl.when(is_end)(end_program)
        pl.when(jnp.logical_not(is_end))(helper_program)
    else:
        line_program()

    for a in range(4):
        for k in range(1, n_head):
            x_copy(a, k).wait_send()
    for src_ref, dst, send, recv, loc in (
        (outc, co, c_send, c_recv, c_loc),
        (outs, so, o_send, o_recv, o_loc),
    ):
        for c in range(nch):
            for k in range(1, n_head):
                cp = out_copy(src_ref, dst, c, k, send, recv)
                cp.wait_send()
                cp.wait_recv()
            local_out(src_ref, dst, c, loc).wait()


def store_kernel(a, b, so, co, sem):
    copies = [
        pltpu.make_async_copy(a, so, sem.at[0]),
        pltpu.make_async_copy(b, co, sem.at[1]),
    ]
    for cp in copies:
        cp.start()
    for cp in copies:
        cp.wait()


def store(a, b):
    return pl.pallas_call(
        store_kernel,
        out_shape=(
            jax.ShapeDtypeStruct(a.shape, a.dtype),
            jax.ShapeDtypeStruct(b.shape, b.dtype),
        ),
        in_specs=[pl.BlockSpec(memory_space=pltpu.VMEM)] * 2,
        out_specs=(pl.BlockSpec(memory_space=pltpu.HBM),) * 2,
        scratch_shapes=[pltpu.SemaphoreType.DMA((2,))],
        compiler_params=pltpu.CompilerParams(vmem_limit_bytes=1024 * 1024),
        name="store_outputs",
    )(a, b)


def per_device(n_patch, n_head, *args):
    fq, fk, fv, sk, sv, cq, tk, tv, mask = args
    rows = fq.shape[1]
    prows = rows * n_head
    hcols = sk.shape[2]
    heads = hcols // HD
    nch = 5 if heads % 5 == 0 else 1
    ccols = hcols // nch
    txt = tk.shape[1]
    peers = max(n_head - 1, 1)
    any_spec = pl.BlockSpec(memory_space=pl.ANY)
    dma = pltpu.SemaphoreType.DMA
    bf16 = jnp.bfloat16
    mixed = pl.pallas_call(
        functools.partial(kernel, n_patch, n_head, nch),
        out_shape=(
            pltpu.VMEM(fq.shape, bf16),
            pltpu.VMEM(cq.shape, bf16),
        ),
        in_specs=[any_spec] * 9,
        out_specs=(pl.BlockSpec(memory_space=pltpu.VMEM),) * 2,
        scratch_shapes=[
            pltpu.VMEM((4, prows, hcols), bf16),
            pltpu.VMEM((n_patch, nch, 2, prows, ccols), bf16),
            pltpu.VMEM((txt, hcols), bf16),
            pltpu.VMEM((txt, hcols), bf16),
            pltpu.VMEM((1, txt), jnp.int32),
            pltpu.VMEM((nch, prows, ccols), bf16),
            pltpu.VMEM((nch, prows, ccols), bf16),
            dma((4, peers)),
            dma((4, peers)),
            dma((4,)),
            dma((3,)),
            dma((nch, 2)),
            dma((2, nch)),
            dma((n_patch, nch)),
            dma((n_patch, nch)),
            dma((nch, peers)),
            dma((nch, peers)),
            dma((nch,)),
            dma((nch, peers)),
            dma((nch, peers)),
            dma((nch,)),
            pltpu.VMEM((prows, hcols), bf16),
            pltpu.VMEM((nch, prows, ccols), bf16),
            pltpu.VMEM((nch, prows, ccols), bf16),
            pltpu.VMEM((nch, prows, HD), jnp.float32),
            pltpu.VMEM((nch, prows, HD), jnp.float32),
            dma((2,)),
            dma((nch, 2)),
            dma((nch, 2)),
        ],
        compiler_params=pltpu.CompilerParams(collective_id=0, has_side_effects=True),
        name="displaced_attention",
    )(*args)
    return store(*mixed)


def solution(mesh):
    return jax.shard_map(
        functools.partial(per_device, mesh.shape["patch"], mesh.shape["head"]),
        mesh=mesh,
        in_specs=(
            P(("group", "cfg"), ("patch", "head"), None),
            P(("group", "cfg"), ("patch", "head"), None),
            P(("group", "cfg"), ("patch", "head"), None),
            P(("group", "cfg"), "patch", "head"),
            P(("group", "cfg"), "patch", "head"),
            P(("group", "cfg"), ("patch", "head"), None),
            P(("group", "cfg"), None, "head"),
            P(("group", "cfg"), None, "head"),
            P(("group", "cfg"), None),
        ),
        out_specs=(
            P(("group", "cfg"), ("patch", "head"), None),
            P(("group", "cfg"), ("patch", "head"), None),
        ),
        check_vma=False,
    )
```

```python
import functools
import math

import jax
import jax.numpy as jnp
from jax import lax
from jax.experimental import pallas as pl
from jax.experimental.pallas import tpu as pltpu
from jax.sharding import PartitionSpec as P

HD = 128
MESH = pl.DeviceIdType.MESH


def dot_nt(a, b):
    return lax.dot_general(a, b, (((1,), (1,)), ((), ())), preferred_element_type=jnp.float32)


def kernel(
    n_patch, n_head, nch,
    fq, fk, fv, sk, sv, cq, tk, tv, mask,
    so, co,
    fx, kv, txk, txv, mk, outs, outc,
    x_send, x_recv, x_loc, t_loc, kv_loc, own_send, fwd_send, kv_recv,
    o_send, o_recv, o_loc, c_send, c_recv, c_loc,
    dq, part_out, part_in, stat_out, stat_in, dq_sem, part_send, part_recv,
):
    p = lax.axis_index("patch")
    h = lax.axis_index("head")
    rows = fq.shape[1]
    prows = rows * n_head
    hcols = sk.shape[2]
    ccols = hcols // nch
    heads = hcols // HD
    cheads = heads // nch
    scale = 1.0 / math.sqrt(HD)
    fresh = (cq, fq, fk, fv)
    my_rows = pl.ds(pl.multiple_of(h * rows, rows), rows)

    for c in range(nch):
        for i, ref in enumerate((sk, sv)):
            pltpu.make_async_copy(
                ref.at[0, :, pl.ds(c * ccols, ccols)], kv.at[p, c, i], kv_loc.at[c, i]
            ).start()
    text_copies = [
        pltpu.make_async_copy(mask, mk, t_loc.at[0]),
        pltpu.make_async_copy(tk.at[0], txk, t_loc.at[1]),
        pltpu.make_async_copy(tv.at[0], txv, t_loc.at[2]),
    ]
    own_copies = [
        pltpu.make_async_copy(
            ref.at[0, :, pl.ds(pl.multiple_of(h * hcols, hcols), hcols)],
            fx.at[a, my_rows, :],
            x_loc.at[a],
        )
        for a, ref in enumerate(fresh)
    ]
    for cp in own_copies + text_copies:
        cp.start()

    barrier = pltpu.get_barrier_semaphore()
    has_right = p < n_patch - 1
    has_left = p > 0

    @pl.when(has_right)
    def _():
        pl.semaphore_signal(barrier, inc=1, device_id={"patch": p + 1}, device_id_type=MESH)

    @pl.when(has_left)
    def _():
        pl.semaphore_signal(barrier, inc=1, device_id={"patch": p - 1}, device_id_type=MESH)

    for k in range(1, n_head):
        pl.semaphore_signal(
            barrier, inc=1, device_id={"head": lax.rem(h + k, n_head)}, device_id_type=MESH
        )
    pl.semaphore_wait(
        barrier, n_head - 1 + has_right.astype(jnp.int32) + has_left.astype(jnp.int32)
    )

    def x_copy(a, k):
        peer = lax.rem(h + k, n_head)
        return pltpu.make_async_remote_copy(
            src_ref=fresh[a].at[0, :, pl.ds(pl.multiple_of(peer * hcols, hcols), hcols)],
            dst_ref=fx.at[a, my_rows, :],
            send_sem=x_send.at[a, k - 1],
            recv_sem=x_recv.at[a, k - 1],
            device_id={"head": peer},
            device_id_type=MESH,
        )

    def kv_copy(src, c, target, sem):
        return pltpu.make_async_remote_copy(
            src_ref=kv.at[src, c],
            dst_ref=kv.at[src, c],
            send_sem=sem,
            recv_sem=kv_recv.at[src, c],
            device_id={"patch": target},
            device_id_type=MESH,
        )

    for a in (1, 0, 2, 3):
        for k in range(1, n_head):
            x_copy(a, k).start()

    def wait_own_kv(c):
        for i, ref in enumerate((sk, sv)):
            pltpu.make_async_copy(
                ref.at[0, :, pl.ds(c * ccols, ccols)], kv.at[p, c, i], kv_loc.at[c, i]
            ).wait()

    def wait_x(a):
        own_copies[a].wait()
        for k in range(1, n_head):
            x_copy(a, k).wait_recv()

    def out_copy(src, dst, c, k, send, recv):
        peer = lax.rem(h + k, n_head)
        return pltpu.make_async_remote_copy(
            src_ref=src.at[c, pl.ds(pl.multiple_of(peer * rows, rows), rows), :],
            dst_ref=dst.at[0, :, pl.ds(pl.multiple_of(h * hcols + c * ccols, HD), ccols)],
            send_sem=send.at[c, k - 1],
            recv_sem=recv.at[c, k - 1],
            device_id={"head": peer},
            device_id_type=MESH,
        )

    def local_out(src, dst, c, sem):
        return pltpu.make_async_copy(
            src.at[c, my_rows, :],
            dst.at[0, :, pl.ds(pl.multiple_of(h * hcols + c * ccols, HD), ccols)],
            sem.at[c],
        )

    def send_out(src, dst, c, send, recv, loc):
        for k in range(1, n_head):
            out_copy(src, dst, c, k, send, recv).start()
        local_out(src, dst, c, loc).start()

    def cross_chunk(c):
        usable = mk[...] > 0
        for i in range(cheads):
            cols = pl.ds((c * cheads + i) * HD, HD)
            scores = dot_nt(fx[0, :, cols], txk[:, cols]) * scale
            scores = jnp.where(usable, scores, -jnp.inf)
            top = jnp.max(scores, axis=-1, keepdims=True)
            weights = jnp.exp(scores - top)
            total = jnp.sum(weights, axis=-1, keepdims=True)
            mix = jnp.dot(
                weights.astype(jnp.bfloat16), txv[:, cols], preferred_element_type=jnp.float32
            )
            outc[c, :, i * HD : (i + 1) * HD] = (mix / total).astype(jnp.bfloat16)

    def query(j):
        return fx[1, :, pl.ds(j * HD, HD)]

    def weigh(q, keys, values, top=None):
        scores = dot_nt(q, keys) * scale
        new_top = jnp.max(scores, axis=-1, keepdims=True)
        if top is not None:
            new_top = jnp.maximum(top, new_top)
        weights = jnp.exp(scores - new_top).astype(jnp.bfloat16)
        wide = jnp.concatenate([values, jnp.ones_like(values)], axis=1)
        mixed = jnp.dot(weights, wide, preferred_element_type=jnp.float32)
        return new_top, mixed[:, HD:], mixed[:, :HD]

    def absorb_rows(state, q, keys, values):
        top, total, mix = state
        new_top, more_total, more_mix = weigh(q, keys, values, top)
        factor = jnp.exp(top - new_top)
        return new_top, total * factor + more_total, mix * factor + more_mix

    def kv_rows(i, j, *sources):
        c, k = divmod(j, cheads)
        parts = [kv[src, c, i, :, pl.ds(k * HD, HD)] for src in sources]
        return parts[0] if len(parts) == 1 else jnp.concatenate(parts, axis=0)

    def fresh_rows(i, j):
        return fx[2 + i, :, pl.ds(j * HD, HD)]

    def first(j):
        return weigh(query(j), fresh_rows(0, j), fresh_rows(1, j))

    def absorb(state, src, j):
        return absorb_rows(state, query(j), kv_rows(0, j, src), kv_rows(1, j, src))

    def line_program():
        for c in range(nch):
            wait_own_kv(c)

            @pl.when(has_right)
            def _():
                kv_copy(p, c, p + 1, own_send.at[0, c]).start()

            @pl.when(has_left)
            def _():
                kv_copy(p, c, p - 1, own_send.at[1, c]).start()

        shorter = jnp.minimum(p, n_patch - 1 - p)

        def slot_source(s):
            near = s // 2 + 1
            near_src = jnp.where(s % 2 == 0, p - near, p + near)
            far = s - shorter + 1
            far_src = jnp.where(p > shorter, p - far, p + far)
            return jnp.where(s < 2 * shorter, near_src, far_src)

        def forward_target(src):
            target = jnp.where(src < p, p + 1, p - 1)
            return target, (target >= 0) & (target < n_patch)

        def forward(s, c):
            src = slot_source(s)
            kv_copy(src, c, p, fwd_send.at[s, c]).wait_recv()
            target, valid = forward_target(src)

            @pl.when(valid)
            def _():
                kv_copy(src, c, target, fwd_send.at[s, c]).start()

        half = (nch + 1) // 2
        for cp in text_copies:
            cp.wait()
        wait_x(0)
        for c in range(half):
            cross_chunk(c)
        for c in range(half):
            forward(0, c)
        for c in range(half, nch):
            cross_chunk(c)
        for c in range(nch):
            send_out(outc, co, c, c_send, c_recv, c_loc)
        for c in range(half, nch):
            forward(0, c)
        for a in range(1, 4):
            wait_x(a)
        states = [first(j) for j in range(heads)]
        src = slot_source(0)
        states = [absorb(states[j], src, j) for j in range(heads)]

        def slot(s, states):
            src = slot_source(s)
            out = []
            for c in range(nch):
                forward(s, c)
                for j in range(c * cheads, (c + 1) * cheads):
                    out.append(absorb(states[j], src, j))
            return out

        if n_patch <= 8:
            for s in range(1, n_patch - 2):
                states = slot(s, states)
        else:
            states = lax.fori_loop(1, n_patch - 2, slot, states)
        last = n_patch - 2
        src = slot_source(last)
        for c in range(nch):
            if last > 0:
                forward(last, c)
            for i in range(cheads):
                j = c * cheads + i
                _, total, mix = absorb(states[j], src, j) if last > 0 else states[j]
                outs[c, :, i * HD : (i + 1) * HD] = (mix / total).astype(jnp.bfloat16)
            if c > 0:
                send_out(outs, so, c - 1, o_send, o_recv, o_loc)
        send_out(outs, so, nch - 1, o_send, o_recv, o_loc)

        for c in range(nch):

            @pl.when(has_right)
            def _():
                kv_copy(p, c, p + 1, own_send.at[0, c]).wait_send()

            @pl.when(has_left)
            def _():
                kv_copy(p, c, p - 1, own_send.at[1, c]).wait_send()

        def drain(s, carry):
            for c in range(nch):
                target, valid = forward_target(slot_source(s))

                @pl.when(valid)
                def _():
                    kv_copy(slot_source(s), c, target, fwd_send.at[s, c]).wait_send()

            return carry

        if n_patch <= 8:
            for s in range(n_patch - 1):
                drain(s, 0)
        else:
            lax.fori_loop(0, n_patch - 1, drain, 0)

    is_end = jnp.logical_not(has_right & has_left)
    across = n_patch - 1 - p
    lanes = lax.broadcasted_iota(jnp.int32, (prows, HD), 1)

    def neighbour(c, other):
        return [
            pltpu.make_async_remote_copy(
                src_ref=src.at[c],
                dst_ref=dst.at[c],
                send_sem=part_send.at[c, i],
                recv_sem=part_recv.at[c, i],
                device_id={"patch": other},
                device_id_type=MESH,
            )
            for i, (src, dst) in enumerate(((part_out, part_in), (stat_out, stat_in)))
        ]

    def dq_copy(other):
        return pltpu.make_async_remote_copy(
            src_ref=fx.at[1],
            dst_ref=dq,
            send_sem=dq_sem.at[0],
            recv_sem=dq_sem.at[1],
            device_id={"patch": other},
            device_id_type=MESH,
        )

    def end_program():
        helper = jnp.where(has_right, p + 1, p - 1)
        lead = min(2, nch)
        for c in range(lead):
            wait_own_kv(c)
            kv_copy(p, c, helper, own_send.at[0, c]).start()
        wait_x(1)
        dq_copy(helper).start()
        for c in range(lead, nch):
            wait_own_kv(c)
            kv_copy(p, c, helper, own_send.at[0, c]).start()
        for cp in text_copies:
            cp.wait()
        wait_x(0)
        for c in range(nch):
            cross_chunk(c)
            if c > 0:
                send_out(outc, co, c - 1, c_send, c_recv, c_loc)
        send_out(outc, co, nch - 1, c_send, c_recv, c_loc)
        wait_x(2)
        wait_x(3)
        states = [first(j) for j in range(heads)]
        for c in range(nch):
            for cp in neighbour(c, helper):
                cp.wait_recv()
            for i in range(cheads):
                top, total, mix = states[c * cheads + i]
                cols = slice(i * HD, (i + 1) * HD)
                lse = stat_in[c, :, i : i + 1]
                new_top = jnp.maximum(top, lse)
                mine = jnp.exp(top - new_top)
                theirs = jnp.exp(lse - new_top)
                mix = mix * mine + part_in[c, :, cols].astype(jnp.float32) * theirs
                outs[c, :, cols] = (mix / (total * mine + theirs)).astype(jnp.bfloat16)
            send_out(outs, so, c, o_send, o_recv, o_loc)
        for c in range(nch):
            kv_copy(p, c, helper, own_send.at[0, c]).wait_send()
        dq_copy(helper).wait_send()

    def helper_program():
        end = jnp.where(p < across, p - 1, p + 1)
        far = n_patch - 1 - end
        for c in range(nch):
            wait_own_kv(c)
            kv_copy(p, c, across, own_send.at[0, c]).start()

        def pass_on(c):
            kv_copy(end, c, across, fwd_send.at[0, c]).wait_recv()
            kv_copy(end, c, across, fwd_send.at[0, c]).start()

        pass_on(0)
        for cp in text_copies:
            cp.wait()
        wait_x(0)
        for c in range(nch):
            cross_chunk(c)
            if c > 0:
                send_out(outc, co, c - 1, c_send, c_recv, c_loc)
            if c + 1 < nch:
                pass_on(c + 1)
        send_out(outc, co, nch - 1, c_send, c_recv, c_loc)
        for a in range(1, 4):
            wait_x(a)
        dq_copy(end).wait_recv()

        def both(j):
            return jnp.concatenate([query(j), dq[:, pl.ds(j * HD, HD)]], axis=0)

        states = []
        for j in range(heads):
            mine = weigh(
                query(j),
                jnp.concatenate([fresh_rows(0, j), kv_rows(0, j, end)], axis=0),
                jnp.concatenate([fresh_rows(1, j), kv_rows(1, j, end)], axis=0),
            )
            theirs = weigh(dq[:, pl.ds(j * HD, HD)], kv_rows(0, j, p), kv_rows(1, j, p))
            states.append([jnp.concatenate(pair, axis=0) for pair in zip(mine, theirs)])
        for c in range(nch):
            kv_copy(across, c, p, own_send.at[0, c]).wait_recv()
        for c in range(nch):
            kv_copy(far, c, p, own_send.at[0, c]).wait_recv()
            stat = jnp.zeros((prows, HD), jnp.float32)
            for i in range(cheads):
                j = c * cheads + i
                top, total, mix = absorb_rows(
                    states[j], both(j), kv_rows(0, j, across, far), kv_rows(1, j, across, far)
                )
                mixed = (mix / total).astype(jnp.bfloat16)
                lse = top[prows:] + jnp.log(total[prows:])
                stat = jnp.where(lanes == i, lse, stat)
                part_out[c, :, i * HD : (i + 1) * HD] = mixed[prows:]
                outs[c, :, i * HD : (i + 1) * HD] = mixed[:prows]
            stat_out[c] = stat
            for cp in neighbour(c, end):
                cp.start()
            send_out(outs, so, c, o_send, o_recv, o_loc)
        for c in range(nch):
            kv_copy(p, c, across, own_send.at[0, c]).wait_send()
            kv_copy(end, c, across, fwd_send.at[0, c]).wait_send()
            for cp in neighbour(c, end):
                cp.wait_send()

    if n_patch == 4:
        pl.when(is_end)(end_program)
        pl.when(jnp.logical_not(is_end))(helper_program)
    else:
        line_program()

    for a in range(4):
        for k in range(1, n_head):
            x_copy(a, k).wait_send()
    for src_ref, dst, send, recv, loc in (
        (outc, co, c_send, c_recv, c_loc),
        (outs, so, o_send, o_recv, o_loc),
    ):
        for c in range(nch):
            for k in range(1, n_head):
                cp = out_copy(src_ref, dst, c, k, send, recv)
                cp.wait_send()
                cp.wait_recv()
            local_out(src_ref, dst, c, loc).wait()


def store_kernel(a, b, so, co, sem):
    copies = [
        pltpu.make_async_copy(a, so, sem.at[0]),
        pltpu.make_async_copy(b, co, sem.at[1]),
    ]
    for cp in copies:
        cp.start()
    for cp in copies:
        cp.wait()


def store(a, b):
    return pl.pallas_call(
        store_kernel,
        out_shape=(
            jax.ShapeDtypeStruct(a.shape, a.dtype),
            jax.ShapeDtypeStruct(b.shape, b.dtype),
        ),
        in_specs=[pl.BlockSpec(memory_space=pltpu.VMEM)] * 2,
        out_specs=(pl.BlockSpec(memory_space=pltpu.HBM),) * 2,
        scratch_shapes=[pltpu.SemaphoreType.DMA((2,))],
        compiler_params=pltpu.CompilerParams(vmem_limit_bytes=1024 * 1024),
        name="store_outputs",
    )(a, b)


def per_device(n_patch, n_head, *args):
    fq, fk, fv, sk, sv, cq, tk, tv, mask = args
    rows = fq.shape[1]
    prows = rows * n_head
    hcols = sk.shape[2]
    heads = hcols // HD
    nch = 5 if heads % 5 == 0 else 1
    ccols = hcols // nch
    txt = tk.shape[1]
    peers = max(n_head - 1, 1)
    any_spec = pl.BlockSpec(memory_space=pl.ANY)
    dma = pltpu.SemaphoreType.DMA
    bf16 = jnp.bfloat16
    mixed = pl.pallas_call(
        functools.partial(kernel, n_patch, n_head, nch),
        out_shape=(
            pltpu.VMEM(fq.shape, bf16),
            pltpu.VMEM(cq.shape, bf16),
        ),
        in_specs=[any_spec] * 9,
        out_specs=(pl.BlockSpec(memory_space=pltpu.VMEM),) * 2,
        scratch_shapes=[
            pltpu.VMEM((4, prows, hcols), bf16),
            pltpu.VMEM((n_patch, nch, 2, prows, ccols), bf16),
            pltpu.VMEM((txt, hcols), bf16),
            pltpu.VMEM((txt, hcols), bf16),
            pltpu.VMEM((1, txt), jnp.int32),
            pltpu.VMEM((nch, prows, ccols), bf16),
            pltpu.VMEM((nch, prows, ccols), bf16),
            dma((4, peers)),
            dma((4, peers)),
            dma((4,)),
            dma((3,)),
            dma((nch, 2)),
            dma((2, nch)),
            dma((n_patch, nch)),
            dma((n_patch, nch)),
            dma((nch, peers)),
            dma((nch, peers)),
            dma((nch,)),
            dma((nch, peers)),
            dma((nch, peers)),
            dma((nch,)),
            pltpu.VMEM((prows, hcols), bf16),
            pltpu.VMEM((nch, prows, ccols), bf16),
            pltpu.VMEM((nch, prows, ccols), bf16),
            pltpu.VMEM((nch, prows, HD), jnp.float32),
            pltpu.VMEM((nch, prows, HD), jnp.float32),
            dma((2,)),
            dma((nch, 2)),
            dma((nch, 2)),
        ],
        compiler_params=pltpu.CompilerParams(collective_id=0, has_side_effects=True),
        name="displaced_attention",
    )(*args)
    return store(*mixed)


def solution(mesh):
    return jax.shard_map(
        functools.partial(per_device, mesh.shape["patch"], mesh.shape["head"]),
        mesh=mesh,
        in_specs=(
            P(("group", "cfg"), ("patch", "head"), None),
            P(("group", "cfg"), ("patch", "head"), None),
            P(("group", "cfg"), ("patch", "head"), None),
            P(("group", "cfg"), "patch", "head"),
            P(("group", "cfg"), "patch", "head"),
            P(("group", "cfg"), ("patch", "head"), None),
            P(("group", "cfg"), None, "head"),
            P(("group", "cfg"), None, "head"),
            P(("group", "cfg"), None),
        ),
        out_specs=(
            P(("group", "cfg"), ("patch", "head"), None),
            P(("group", "cfg"), ("patch", "head"), None),
        ),
        check_vma=False,
    )
```

```python
import functools
import math

import jax
import jax.numpy as jnp
from jax import lax
from jax.experimental import pallas as pl
from jax.experimental.pallas import tpu as pltpu
from jax.sharding import PartitionSpec as P

HD = 128
MESH = pl.DeviceIdType.MESH


def dot_nt(a, b):
    return lax.dot_general(a, b, (((1,), (1,)), ((), ())), preferred_element_type=jnp.float32)


def kernel(
    n_patch, n_head, nch,
    fq, fk, fv, sk, sv, cq, tk, tv, mask,
    so, co,
    fx, kv, txk, txv, mk, outs, outc,
    x_send, x_recv, x_loc, t_loc, kv_loc, own_send, fwd_send, kv_recv,
    o_send, o_recv, o_loc, c_send, c_recv, c_loc,
    dq, part_out, part_in, stat_out, stat_in, dq_sem, part_send, part_recv,
):
    p = lax.axis_index("patch")
    h = lax.axis_index("head")
    rows = fq.shape[1]
    prows = rows * n_head
    hcols = sk.shape[2]
    ccols = hcols // nch
    heads = hcols // HD
    cheads = heads // nch
    scale = 1.0 / math.sqrt(HD)
    fresh = (cq, fq, fk, fv)
    my_rows = pl.ds(pl.multiple_of(h * rows, rows), rows)

    for c in range(nch):
        for i, ref in enumerate((sk, sv)):
            pltpu.make_async_copy(
                ref.at[0, :, pl.ds(c * ccols, ccols)], kv.at[p, c, i], kv_loc.at[c, i]
            ).start()
    text_copies = [
        pltpu.make_async_copy(mask, mk, t_loc.at[0]),
        pltpu.make_async_copy(tk.at[0], txk, t_loc.at[1]),
        pltpu.make_async_copy(tv.at[0], txv, t_loc.at[2]),
    ]
    own_copies = [
        pltpu.make_async_copy(
            ref.at[0, :, pl.ds(pl.multiple_of(h * hcols, hcols), hcols)],
            fx.at[a, my_rows, :],
            x_loc.at[a],
        )
        for a, ref in enumerate(fresh)
    ]
    for cp in own_copies + text_copies:
        cp.start()

    barrier = pltpu.get_barrier_semaphore()
    has_right = p < n_patch - 1
    has_left = p > 0

    @pl.when(has_right)
    def _():
        pl.semaphore_signal(barrier, inc=1, device_id={"patch": p + 1}, device_id_type=MESH)

    @pl.when(has_left)
    def _():
        pl.semaphore_signal(barrier, inc=1, device_id={"patch": p - 1}, device_id_type=MESH)

    for k in range(1, n_head):
        pl.semaphore_signal(
            barrier, inc=1, device_id={"head": lax.rem(h + k, n_head)}, device_id_type=MESH
        )
    pl.semaphore_wait(
        barrier, n_head - 1 + has_right.astype(jnp.int32) + has_left.astype(jnp.int32)
    )

    def x_copy(a, k):
        peer = lax.rem(h + k, n_head)
        return pltpu.make_async_remote_copy(
            src_ref=fresh[a].at[0, :, pl.ds(pl.multiple_of(peer * hcols, hcols), hcols)],
            dst_ref=fx.at[a, my_rows, :],
            send_sem=x_send.at[a, k - 1],
            recv_sem=x_recv.at[a, k - 1],
            device_id={"head": peer},
            device_id_type=MESH,
        )

    def kv_copy(src, c, target, sem):
        return pltpu.make_async_remote_copy(
            src_ref=kv.at[src, c],
            dst_ref=kv.at[src, c],
            send_sem=sem,
            recv_sem=kv_recv.at[src, c],
            device_id={"patch": target},
            device_id_type=MESH,
        )

    def start_x():
        for a in (1, 0, 2, 3):
            for k in range(1, n_head):
                x_copy(a, k).start()

    def wait_own_kv(c):
        for i, ref in enumerate((sk, sv)):
            pltpu.make_async_copy(
                ref.at[0, :, pl.ds(c * ccols, ccols)], kv.at[p, c, i], kv_loc.at[c, i]
            ).wait()

    def wait_x(a):
        own_copies[a].wait()
        for k in range(1, n_head):
            x_copy(a, k).wait_recv()

    def out_copy(src, dst, c, k, send, recv):
        peer = lax.rem(h + k, n_head)
        return pltpu.make_async_remote_copy(
            src_ref=src.at[c, pl.ds(pl.multiple_of(peer * rows, rows), rows), :],
            dst_ref=dst.at[0, :, pl.ds(pl.multiple_of(h * hcols + c * ccols, HD), ccols)],
            send_sem=send.at[c, k - 1],
            recv_sem=recv.at[c, k - 1],
            device_id={"head": peer},
            device_id_type=MESH,
        )

    def local_out(src, dst, c, sem):
        return pltpu.make_async_copy(
            src.at[c, my_rows, :],
            dst.at[0, :, pl.ds(pl.multiple_of(h * hcols + c * ccols, HD), ccols)],
            sem.at[c],
        )

    def send_out(src, dst, c, send, recv, loc):
        for k in range(1, n_head):
            out_copy(src, dst, c, k, send, recv).start()
        local_out(src, dst, c, loc).start()

    def cross_chunk(c):
        usable = mk[...] > 0
        for i in range(cheads):
            cols = pl.ds((c * cheads + i) * HD, HD)
            scores = dot_nt(fx[0, :, cols], txk[:, cols]) * scale
            scores = jnp.where(usable, scores, -jnp.inf)
            top = jnp.max(scores, axis=-1, keepdims=True)
            weights = jnp.exp(scores - top)
            total = jnp.sum(weights, axis=-1, keepdims=True)
            mix = jnp.dot(
                weights.astype(jnp.bfloat16), txv[:, cols], preferred_element_type=jnp.float32
            )
            outc[c, :, i * HD : (i + 1) * HD] = (mix / total).astype(jnp.bfloat16)

    def query(j):
        return fx[1, :, pl.ds(j * HD, HD)]

    def weigh(q, keys, values, top=None):
        scores = dot_nt(q, keys) * scale
        new_top = jnp.max(scores, axis=-1, keepdims=True)
        if top is not None:
            new_top = jnp.maximum(top, new_top)
        weights = jnp.exp(scores - new_top).astype(jnp.bfloat16)
        wide = jnp.concatenate([values, jnp.ones_like(values)], axis=1)
        mixed = jnp.dot(weights, wide, preferred_element_type=jnp.float32)
        return new_top, mixed[:, HD:], mixed[:, :HD]

    def absorb_rows(state, q, keys, values):
        top, total, mix = state
        new_top, more_total, more_mix = weigh(q, keys, values, top)
        factor = jnp.exp(top - new_top)
        return new_top, total * factor + more_total, mix * factor + more_mix

    def kv_rows(i, j, *sources):
        c, k = divmod(j, cheads)
        parts = [kv[src, c, i, :, pl.ds(k * HD, HD)] for src in sources]
        return parts[0] if len(parts) == 1 else jnp.concatenate(parts, axis=0)

    def fresh_rows(i, j):
        return fx[2 + i, :, pl.ds(j * HD, HD)]

    def first(j):
        return weigh(query(j), fresh_rows(0, j), fresh_rows(1, j))

    def absorb(state, src, j):
        return absorb_rows(state, query(j), kv_rows(0, j, src), kv_rows(1, j, src))

    def line_program():
        start_x()
        for c in range(nch):
            wait_own_kv(c)

            @pl.when(has_right)
            def _():
                kv_copy(p, c, p + 1, own_send.at[0, c]).start()

            @pl.when(has_left)
            def _():
                kv_copy(p, c, p - 1, own_send.at[1, c]).start()

        shorter = jnp.minimum(p, n_patch - 1 - p)

        def slot_source(s):
            near = s // 2 + 1
            near_src = jnp.where(s % 2 == 0, p - near, p + near)
            far = s - shorter + 1
            far_src = jnp.where(p > shorter, p - far, p + far)
            return jnp.where(s < 2 * shorter, near_src, far_src)

        def forward_target(src):
            target = jnp.where(src < p, p + 1, p - 1)
            return target, (target >= 0) & (target < n_patch)

        def forward(s, c):
            src = slot_source(s)
            kv_copy(src, c, p, fwd_send.at[s, c]).wait_recv()
            target, valid = forward_target(src)

            @pl.when(valid)
            def _():
                kv_copy(src, c, target, fwd_send.at[s, c]).start()

        half = (nch + 1) // 2
        for cp in text_copies:
            cp.wait()
        wait_x(0)
        for c in range(half):
            cross_chunk(c)
        for c in range(half):
            forward(0, c)
        for c in range(half, nch):
            cross_chunk(c)
        for c in range(nch):
            send_out(outc, co, c, c_send, c_recv, c_loc)
        for c in range(half, nch):
            forward(0, c)
        for a in range(1, 4):
            wait_x(a)
        states = [first(j) for j in range(heads)]
        src = slot_source(0)
        states = [absorb(states[j], src, j) for j in range(heads)]

        def slot(s, states):
            src = slot_source(s)
            out = []
            for c in range(nch):
                forward(s, c)
                for j in range(c * cheads, (c + 1) * cheads):
                    out.append(absorb(states[j], src, j))
            return out

        if n_patch <= 8:
            for s in range(1, n_patch - 2):
                states = slot(s, states)
        else:
            states = lax.fori_loop(1, n_patch - 2, slot, states)
        last = n_patch - 2
        src = slot_source(last)
        for c in range(nch):
            if last > 0:
                forward(last, c)
            for i in range(cheads):
                j = c * cheads + i
                _, total, mix = absorb(states[j], src, j) if last > 0 else states[j]
                outs[c, :, i * HD : (i + 1) * HD] = (mix / total).astype(jnp.bfloat16)
            if c > 0:
                send_out(outs, so, c - 1, o_send, o_recv, o_loc)
        send_out(outs, so, nch - 1, o_send, o_recv, o_loc)

        for c in range(nch):

            @pl.when(has_right)
            def _():
                kv_copy(p, c, p + 1, own_send.at[0, c]).wait_send()

            @pl.when(has_left)
            def _():
                kv_copy(p, c, p - 1, own_send.at[1, c]).wait_send()

        def drain(s, carry):
            for c in range(nch):
                target, valid = forward_target(slot_source(s))

                @pl.when(valid)
                def _():
                    kv_copy(slot_source(s), c, target, fwd_send.at[s, c]).wait_send()

            return carry

        if n_patch <= 8:
            for s in range(n_patch - 1):
                drain(s, 0)
        else:
            lax.fori_loop(0, n_patch - 1, drain, 0)

    is_end = jnp.logical_not(has_right & has_left)
    across = n_patch - 1 - p
    lanes = lax.broadcasted_iota(jnp.int32, (prows, HD), 1)

    def neighbour(c, other):
        return [
            pltpu.make_async_remote_copy(
                src_ref=src.at[c],
                dst_ref=dst.at[c],
                send_sem=part_send.at[c, i],
                recv_sem=part_recv.at[c, i],
                device_id={"patch": other},
                device_id_type=MESH,
            )
            for i, (src, dst) in enumerate(((part_out, part_in), (stat_out, stat_in)))
        ]

    def dq_copy(other):
        return pltpu.make_async_remote_copy(
            src_ref=fx.at[1],
            dst_ref=dq,
            send_sem=dq_sem.at[0],
            recv_sem=dq_sem.at[1],
            device_id={"patch": other},
            device_id_type=MESH,
        )

    def end_program():
        helper = jnp.where(has_right, p + 1, p - 1)
        lead = min(2, nch)
        for c in range(lead):
            wait_own_kv(c)
            kv_copy(p, c, helper, own_send.at[0, c]).start()
        start_x()
        wait_x(1)
        dq_copy(helper).start()
        for c in range(lead, nch):
            wait_own_kv(c)
            kv_copy(p, c, helper, own_send.at[0, c]).start()
        for cp in text_copies:
            cp.wait()
        wait_x(0)
        for c in range(nch):
            cross_chunk(c)
            if c > 0:
                send_out(outc, co, c - 1, c_send, c_recv, c_loc)
        send_out(outc, co, nch - 1, c_send, c_recv, c_loc)
        wait_x(2)
        wait_x(3)
        states = [first(j) for j in range(heads)]
        for c in range(nch):
            for cp in neighbour(c, helper):
                cp.wait_recv()
            for i in range(cheads):
                top, total, mix = states[c * cheads + i]
                cols = slice(i * HD, (i + 1) * HD)
                lse = stat_in[c, :, i : i + 1]
                new_top = jnp.maximum(top, lse)
                mine = jnp.exp(top - new_top)
                theirs = jnp.exp(lse - new_top)
                mix = mix * mine + part_in[c, :, cols].astype(jnp.float32) * theirs
                outs[c, :, cols] = (mix / (total * mine + theirs)).astype(jnp.bfloat16)
            send_out(outs, so, c, o_send, o_recv, o_loc)
        for c in range(nch):
            kv_copy(p, c, helper, own_send.at[0, c]).wait_send()
        dq_copy(helper).wait_send()

    def helper_program():
        end = jnp.where(p < across, p - 1, p + 1)
        far = n_patch - 1 - end
        for c in range(nch):
            wait_own_kv(c)
            kv_copy(p, c, across, own_send.at[0, c]).start()

        start_x()

        def pass_on(c):
            kv_copy(end, c, across, fwd_send.at[0, c]).wait_recv()
            kv_copy(end, c, across, fwd_send.at[0, c]).start()

        pass_on(0)
        for cp in text_copies:
            cp.wait()
        wait_x(0)
        for c in range(nch):
            cross_chunk(c)
            if c > 0:
                send_out(outc, co, c - 1, c_send, c_recv, c_loc)
            if c + 1 < nch:
                pass_on(c + 1)
        send_out(outc, co, nch - 1, c_send, c_recv, c_loc)
        for a in range(1, 4):
            wait_x(a)
        dq_copy(end).wait_recv()

        def both(j):
            return jnp.concatenate([query(j), dq[:, pl.ds(j * HD, HD)]], axis=0)

        states = []
        for j in range(heads):
            mine = weigh(
                query(j),
                jnp.concatenate([fresh_rows(0, j), kv_rows(0, j, end)], axis=0),
                jnp.concatenate([fresh_rows(1, j), kv_rows(1, j, end)], axis=0),
            )
            theirs = weigh(dq[:, pl.ds(j * HD, HD)], kv_rows(0, j, p), kv_rows(1, j, p))
            states.append([jnp.concatenate(pair, axis=0) for pair in zip(mine, theirs)])
        for c in range(nch):
            kv_copy(across, c, p, own_send.at[0, c]).wait_recv()
        for c in range(nch):
            kv_copy(far, c, p, own_send.at[0, c]).wait_recv()
            stat = jnp.zeros((prows, HD), jnp.float32)
            for i in range(cheads):
                j = c * cheads + i
                top, total, mix = absorb_rows(
                    states[j], both(j), kv_rows(0, j, across, far), kv_rows(1, j, across, far)
                )
                mixed = (mix / total).astype(jnp.bfloat16)
                lse = top[prows:] + jnp.log(total[prows:])
                stat = jnp.where(lanes == i, lse, stat)
                part_out[c, :, i * HD : (i + 1) * HD] = mixed[prows:]
                outs[c, :, i * HD : (i + 1) * HD] = mixed[:prows]
            stat_out[c] = stat
            for cp in neighbour(c, end):
                cp.start()
            send_out(outs, so, c, o_send, o_recv, o_loc)
        for c in range(nch):
            kv_copy(p, c, across, own_send.at[0, c]).wait_send()
            kv_copy(end, c, across, fwd_send.at[0, c]).wait_send()
            for cp in neighbour(c, end):
                cp.wait_send()

    if n_patch == 4:
        pl.when(is_end)(end_program)
        pl.when(jnp.logical_not(is_end))(helper_program)
    else:
        line_program()

    for a in range(4):
        for k in range(1, n_head):
            x_copy(a, k).wait_send()
    for src_ref, dst, send, recv, loc in (
        (outc, co, c_send, c_recv, c_loc),
        (outs, so, o_send, o_recv, o_loc),
    ):
        for c in range(nch):
            for k in range(1, n_head):
                cp = out_copy(src_ref, dst, c, k, send, recv)
                cp.wait_send()
                cp.wait_recv()
            local_out(src_ref, dst, c, loc).wait()


def store_kernel(a, b, so, co, sem):
    copies = [
        pltpu.make_async_copy(a, so, sem.at[0]),
        pltpu.make_async_copy(b, co, sem.at[1]),
    ]
    for cp in copies:
        cp.start()
    for cp in copies:
        cp.wait()


def store(a, b):
    return pl.pallas_call(
        store_kernel,
        out_shape=(
            jax.ShapeDtypeStruct(a.shape, a.dtype),
            jax.ShapeDtypeStruct(b.shape, b.dtype),
        ),
        in_specs=[pl.BlockSpec(memory_space=pltpu.VMEM)] * 2,
        out_specs=(pl.BlockSpec(memory_space=pltpu.HBM),) * 2,
        scratch_shapes=[pltpu.SemaphoreType.DMA((2,))],
        compiler_params=pltpu.CompilerParams(vmem_limit_bytes=1024 * 1024),
        name="store_outputs",
    )(a, b)


def per_device(n_patch, n_head, *args):
    fq, fk, fv, sk, sv, cq, tk, tv, mask = args
    rows = fq.shape[1]
    prows = rows * n_head
    hcols = sk.shape[2]
    heads = hcols // HD
    nch = 2 if heads % 2 == 0 else 1
    ccols = hcols // nch
    txt = tk.shape[1]
    peers = max(n_head - 1, 1)
    any_spec = pl.BlockSpec(memory_space=pl.ANY)
    dma = pltpu.SemaphoreType.DMA
    bf16 = jnp.bfloat16
    mixed = pl.pallas_call(
        functools.partial(kernel, n_patch, n_head, nch),
        out_shape=(
            pltpu.VMEM(fq.shape, bf16),
            pltpu.VMEM(cq.shape, bf16),
        ),
        in_specs=[any_spec] * 9,
        out_specs=(pl.BlockSpec(memory_space=pltpu.VMEM),) * 2,
        scratch_shapes=[
            pltpu.VMEM((4, prows, hcols), bf16),
            pltpu.VMEM((n_patch, nch, 2, prows, ccols), bf16),
            pltpu.VMEM((txt, hcols), bf16),
            pltpu.VMEM((txt, hcols), bf16),
            pltpu.VMEM((1, txt), jnp.int32),
            pltpu.VMEM((nch, prows, ccols), bf16),
            pltpu.VMEM((nch, prows, ccols), bf16),
            dma((4, peers)),
            dma((4, peers)),
            dma((4,)),
            dma((3,)),
            dma((nch, 2)),
            dma((2, nch)),
            dma((n_patch, nch)),
            dma((n_patch, nch)),
            dma((nch, peers)),
            dma((nch, peers)),
            dma((nch,)),
            dma((nch, peers)),
            dma((nch, peers)),
            dma((nch,)),
            pltpu.VMEM((prows, hcols), bf16),
            pltpu.VMEM((nch, prows, ccols), bf16),
            pltpu.VMEM((nch, prows, ccols), bf16),
            pltpu.VMEM((nch, prows, HD), jnp.float32),
            pltpu.VMEM((nch, prows, HD), jnp.float32),
            dma((2,)),
            dma((nch, 2)),
            dma((nch, 2)),
        ],
        compiler_params=pltpu.CompilerParams(collective_id=0, has_side_effects=True),
        name="displaced_attention",
    )(*args)
    return store(*mixed)


def solution(mesh):
    return jax.shard_map(
        functools.partial(per_device, mesh.shape["patch"], mesh.shape["head"]),
        mesh=mesh,
        in_specs=(
            P(("group", "cfg"), ("patch", "head"), None),
            P(("group", "cfg"), ("patch", "head"), None),
            P(("group", "cfg"), ("patch", "head"), None),
            P(("group", "cfg"), "patch", "head"),
            P(("group", "cfg"), "patch", "head"),
            P(("group", "cfg"), ("patch", "head"), None),
            P(("group", "cfg"), None, "head"),
            P(("group", "cfg"), None, "head"),
            P(("group", "cfg"), None),
        ),
        out_specs=(
            P(("group", "cfg"), ("patch", "head"), None),
            P(("group", "cfg"), ("patch", "head"), None),
        ),
        check_vma=False,
    )
```

```python
import functools
import math

import jax
import jax.numpy as jnp
from jax import lax
from jax.experimental import pallas as pl
from jax.experimental.pallas import tpu as pltpu
from jax.sharding import PartitionSpec as P

HD = 128
MESH = pl.DeviceIdType.MESH


def dot_nt(a, b):
    return lax.dot_general(a, b, (((1,), (1,)), ((), ())), preferred_element_type=jnp.float32)


def kernel(
    n_patch, n_head, nch,
    fq, fk, fv, sk, sv, cq, tk, tv, mask,
    so, co,
    fx, kv, txk, txv, mk, outs, outc,
    x_send, x_recv, x_loc, t_loc, kv_loc, own_send, fwd_send, kv_recv,
    o_send, o_recv, o_loc, c_send, c_recv, c_loc,
    dq, part_out, part_in, stat_out, stat_in, dq_sem, part_send, part_recv,
):
    p = lax.axis_index("patch")
    h = lax.axis_index("head")
    rows = fq.shape[1]
    prows = rows * n_head
    hcols = sk.shape[2]
    ccols = hcols // nch
    heads = hcols // HD
    cheads = heads // nch
    scale = 1.0 / math.sqrt(HD)
    fresh = (cq, fq, fk, fv)
    my_rows = pl.ds(pl.multiple_of(h * rows, rows), rows)

    for c in range(nch):
        for i, ref in enumerate((sk, sv)):
            pltpu.make_async_copy(
                ref.at[0, :, pl.ds(c * ccols, ccols)], kv.at[p, c, i], kv_loc.at[c, i]
            ).start()
    text_copies = [
        pltpu.make_async_copy(mask, mk, t_loc.at[0]),
        pltpu.make_async_copy(tk.at[0], txk, t_loc.at[1]),
        pltpu.make_async_copy(tv.at[0], txv, t_loc.at[2]),
    ]
    own_copies = [
        pltpu.make_async_copy(
            ref.at[0, :, pl.ds(pl.multiple_of(h * hcols, hcols), hcols)],
            fx.at[a, my_rows, :],
            x_loc.at[a],
        )
        for a, ref in enumerate(fresh)
    ]
    for cp in own_copies + text_copies:
        cp.start()

    barrier = pltpu.get_barrier_semaphore()
    has_right = p < n_patch - 1
    has_left = p > 0

    @pl.when(has_right)
    def _():
        pl.semaphore_signal(barrier, inc=1, device_id={"patch": p + 1}, device_id_type=MESH)

    @pl.when(has_left)
    def _():
        pl.semaphore_signal(barrier, inc=1, device_id={"patch": p - 1}, device_id_type=MESH)

    for k in range(1, n_head):
        pl.semaphore_signal(
            barrier, inc=1, device_id={"head": lax.rem(h + k, n_head)}, device_id_type=MESH
        )
    pl.semaphore_wait(
        barrier, n_head - 1 + has_right.astype(jnp.int32) + has_left.astype(jnp.int32)
    )

    def x_copy(a, k):
        peer = lax.rem(h + k, n_head)
        return pltpu.make_async_remote_copy(
            src_ref=fresh[a].at[0, :, pl.ds(pl.multiple_of(peer * hcols, hcols), hcols)],
            dst_ref=fx.at[a, my_rows, :],
            send_sem=x_send.at[a, k - 1],
            recv_sem=x_recv.at[a, k - 1],
            device_id={"head": peer},
            device_id_type=MESH,
        )

    def kv_copy(src, c, target, sem):
        return pltpu.make_async_remote_copy(
            src_ref=kv.at[src, c],
            dst_ref=kv.at[src, c],
            send_sem=sem,
            recv_sem=kv_recv.at[src, c],
            device_id={"patch": target},
            device_id_type=MESH,
        )

    def start_x():
        for a in (1, 0, 2, 3):
            for k in range(1, n_head):
                x_copy(a, k).start()

    def wait_own_kv(c):
        for i, ref in enumerate((sk, sv)):
            pltpu.make_async_copy(
                ref.at[0, :, pl.ds(c * ccols, ccols)], kv.at[p, c, i], kv_loc.at[c, i]
            ).wait()

    def wait_x(a):
        own_copies[a].wait()
        for k in range(1, n_head):
            x_copy(a, k).wait_recv()

    def out_copy(src, dst, c, k, send, recv):
        peer = lax.rem(h + k, n_head)
        return pltpu.make_async_remote_copy(
            src_ref=src.at[c, pl.ds(pl.multiple_of(peer * rows, rows), rows), :],
            dst_ref=dst.at[0, :, pl.ds(pl.multiple_of(h * hcols + c * ccols, HD), ccols)],
            send_sem=send.at[c, k - 1],
            recv_sem=recv.at[c, k - 1],
            device_id={"head": peer},
            device_id_type=MESH,
        )

    def local_out(src, dst, c, sem):
        return pltpu.make_async_copy(
            src.at[c, my_rows, :],
            dst.at[0, :, pl.ds(pl.multiple_of(h * hcols + c * ccols, HD), ccols)],
            sem.at[c],
        )

    def send_out(src, dst, c, send, recv, loc):
        for k in range(1, n_head):
            out_copy(src, dst, c, k, send, recv).start()
        local_out(src, dst, c, loc).start()

    def cross_chunk(c):
        usable = mk[...] > 0
        for i in range(cheads):
            cols = pl.ds((c * cheads + i) * HD, HD)
            scores = dot_nt(fx[0, :, cols], txk[:, cols]) * scale
            scores = jnp.where(usable, scores, -jnp.inf)
            top = jnp.max(scores, axis=-1, keepdims=True)
            weights = jnp.exp(scores - top)
            total = jnp.sum(weights, axis=-1, keepdims=True)
            mix = jnp.dot(
                weights.astype(jnp.bfloat16), txv[:, cols], preferred_element_type=jnp.float32
            )
            outc[c, :, i * HD : (i + 1) * HD] = (mix / total).astype(jnp.bfloat16)

    def query(j):
        return fx[1, :, pl.ds(j * HD, HD)]

    def weigh(q, keys, values, top=None):
        scores = dot_nt(q, keys) * scale
        new_top = jnp.max(scores, axis=-1, keepdims=True)
        if top is not None:
            new_top = jnp.maximum(top, new_top)
        weights = jnp.exp(scores - new_top).astype(jnp.bfloat16)
        wide = jnp.concatenate([values, jnp.ones_like(values)], axis=1)
        mixed = jnp.dot(weights, wide, preferred_element_type=jnp.float32)
        return new_top, mixed[:, HD:], mixed[:, :HD]

    def absorb_rows(state, q, keys, values):
        top, total, mix = state
        new_top, more_total, more_mix = weigh(q, keys, values, top)
        factor = jnp.exp(top - new_top)
        return new_top, total * factor + more_total, mix * factor + more_mix

    def kv_rows(i, j, *sources):
        c, k = divmod(j, cheads)
        parts = [kv[src, c, i, :, pl.ds(k * HD, HD)] for src in sources]
        return parts[0] if len(parts) == 1 else jnp.concatenate(parts, axis=0)

    def fresh_rows(i, j):
        return fx[2 + i, :, pl.ds(j * HD, HD)]

    def first(j):
        return weigh(query(j), fresh_rows(0, j), fresh_rows(1, j))

    def absorb(state, src, j):
        return absorb_rows(state, query(j), kv_rows(0, j, src), kv_rows(1, j, src))

    def line_program():
        start_x()
        for c in range(nch):
            wait_own_kv(c)

            @pl.when(has_right)
            def _():
                kv_copy(p, c, p + 1, own_send.at[0, c]).start()

            @pl.when(has_left)
            def _():
                kv_copy(p, c, p - 1, own_send.at[1, c]).start()

        shorter = jnp.minimum(p, n_patch - 1 - p)

        def slot_source(s):
            near = s // 2 + 1
            near_src = jnp.where(s % 2 == 0, p - near, p + near)
            far = s - shorter + 1
            far_src = jnp.where(p > shorter, p - far, p + far)
            return jnp.where(s < 2 * shorter, near_src, far_src)

        def forward_target(src):
            target = jnp.where(src < p, p + 1, p - 1)
            return target, (target >= 0) & (target < n_patch)

        def forward(s, c):
            src = slot_source(s)
            kv_copy(src, c, p, fwd_send.at[s, c]).wait_recv()
            target, valid = forward_target(src)

            @pl.when(valid)
            def _():
                kv_copy(src, c, target, fwd_send.at[s, c]).start()

        half = (nch + 1) // 2
        for cp in text_copies:
            cp.wait()
        wait_x(0)
        for c in range(half):
            cross_chunk(c)
        for c in range(half):
            forward(0, c)
        for c in range(half, nch):
            cross_chunk(c)
        for c in range(nch):
            send_out(outc, co, c, c_send, c_recv, c_loc)
        for c in range(half, nch):
            forward(0, c)
        for a in range(1, 4):
            wait_x(a)
        states = [first(j) for j in range(heads)]
        src = slot_source(0)
        states = [absorb(states[j], src, j) for j in range(heads)]

        def slot(s, states):
            src = slot_source(s)
            out = []
            for c in range(nch):
                forward(s, c)
                for j in range(c * cheads, (c + 1) * cheads):
                    out.append(absorb(states[j], src, j))
            return out

        if n_patch <= 8:
            for s in range(1, n_patch - 2):
                states = slot(s, states)
        else:
            states = lax.fori_loop(1, n_patch - 2, slot, states)
        last = n_patch - 2
        src = slot_source(last)
        for c in range(nch):
            if last > 0:
                forward(last, c)
            for i in range(cheads):
                j = c * cheads + i
                _, total, mix = absorb(states[j], src, j) if last > 0 else states[j]
                outs[c, :, i * HD : (i + 1) * HD] = (mix / total).astype(jnp.bfloat16)
            if c > 0:
                send_out(outs, so, c - 1, o_send, o_recv, o_loc)
        send_out(outs, so, nch - 1, o_send, o_recv, o_loc)

        for c in range(nch):

            @pl.when(has_right)
            def _():
                kv_copy(p, c, p + 1, own_send.at[0, c]).wait_send()

            @pl.when(has_left)
            def _():
                kv_copy(p, c, p - 1, own_send.at[1, c]).wait_send()

        def drain(s, carry):
            for c in range(nch):
                target, valid = forward_target(slot_source(s))

                @pl.when(valid)
                def _():
                    kv_copy(slot_source(s), c, target, fwd_send.at[s, c]).wait_send()

            return carry

        if n_patch <= 8:
            for s in range(n_patch - 1):
                drain(s, 0)
        else:
            lax.fori_loop(0, n_patch - 1, drain, 0)

    is_end = jnp.logical_not(has_right & has_left)
    across = n_patch - 1 - p
    lanes = lax.broadcasted_iota(jnp.int32, (prows, HD), 1)

    early = (cheads + 1) // 2

    def neighbour(c, other):
        return [
            pltpu.make_async_remote_copy(
                src_ref=src.at[c, :, pl.ds(at, size)],
                dst_ref=dst.at[c, :, pl.ds(at, size)],
                send_sem=part_send.at[c, i],
                recv_sem=part_recv.at[c, i],
                device_id={"patch": other},
                device_id_type=MESH,
            )
            for i, (src, dst, at, size) in enumerate(
                (
                    (part_out, part_in, 0, early * HD),
                    (part_out, part_in, early * HD, (cheads - early) * HD),
                    (stat_out, stat_in, 0, HD),
                )
            )
        ]

    def dq_copy(other):
        return pltpu.make_async_remote_copy(
            src_ref=fx.at[1],
            dst_ref=dq,
            send_sem=dq_sem.at[0],
            recv_sem=dq_sem.at[1],
            device_id={"patch": other},
            device_id_type=MESH,
        )

    def end_program():
        helper = jnp.where(has_right, p + 1, p - 1)
        lead = min(2, nch)
        for c in range(lead):
            wait_own_kv(c)
            kv_copy(p, c, helper, own_send.at[0, c]).start()
        start_x()
        wait_x(1)
        dq_copy(helper).start()
        for c in range(lead, nch):
            wait_own_kv(c)
            kv_copy(p, c, helper, own_send.at[0, c]).start()
        for cp in text_copies:
            cp.wait()
        wait_x(0)
        for c in range(nch):
            cross_chunk(c)
            if c > 0:
                send_out(outc, co, c - 1, c_send, c_recv, c_loc)
        send_out(outc, co, nch - 1, c_send, c_recv, c_loc)
        wait_x(2)
        wait_x(3)
        states = [first(j) for j in range(heads)]
        for c in range(nch):
            for cp in neighbour(c, helper):
                cp.wait_recv()
            for i in range(cheads):
                top, total, mix = states[c * cheads + i]
                cols = slice(i * HD, (i + 1) * HD)
                lse = stat_in[c, :, i : i + 1]
                new_top = jnp.maximum(top, lse)
                mine = jnp.exp(top - new_top)
                theirs = jnp.exp(lse - new_top)
                mix = mix * mine + part_in[c, :, cols].astype(jnp.float32) * theirs
                outs[c, :, cols] = (mix / (total * mine + theirs)).astype(jnp.bfloat16)
            send_out(outs, so, c, o_send, o_recv, o_loc)
        for c in range(nch):
            kv_copy(p, c, helper, own_send.at[0, c]).wait_send()
        dq_copy(helper).wait_send()

    def helper_program():
        end = jnp.where(p < across, p - 1, p + 1)
        far = n_patch - 1 - end
        for c in range(nch):
            wait_own_kv(c)
            kv_copy(p, c, across, own_send.at[0, c]).start()

        start_x()

        def pass_on(c):
            kv_copy(end, c, across, fwd_send.at[0, c]).wait_recv()
            kv_copy(end, c, across, fwd_send.at[0, c]).start()

        pass_on(0)
        for cp in text_copies:
            cp.wait()
        wait_x(0)
        for c in range(nch):
            cross_chunk(c)
            if c > 0:
                send_out(outc, co, c - 1, c_send, c_recv, c_loc)
            if c + 1 < nch:
                pass_on(c + 1)
        send_out(outc, co, nch - 1, c_send, c_recv, c_loc)
        for a in range(1, 4):
            wait_x(a)
        dq_copy(end).wait_recv()

        def both(j):
            return jnp.concatenate([query(j), dq[:, pl.ds(j * HD, HD)]], axis=0)

        states = []
        for j in range(heads):
            mine = weigh(
                query(j),
                jnp.concatenate([fresh_rows(0, j), kv_rows(0, j, end)], axis=0),
                jnp.concatenate([fresh_rows(1, j), kv_rows(1, j, end)], axis=0),
            )
            theirs = weigh(dq[:, pl.ds(j * HD, HD)], kv_rows(0, j, p), kv_rows(1, j, p))
            states.append([jnp.concatenate(pair, axis=0) for pair in zip(mine, theirs)])
        for c in range(nch):
            kv_copy(across, c, p, own_send.at[0, c]).wait_recv()
        for c in range(nch):
            kv_copy(far, c, p, own_send.at[0, c]).wait_recv()
            stat = jnp.zeros((prows, HD), jnp.float32)
            for i in range(cheads):
                j = c * cheads + i
                top, total, mix = absorb_rows(
                    states[j], both(j), kv_rows(0, j, across, far), kv_rows(1, j, across, far)
                )
                mixed = (mix / total).astype(jnp.bfloat16)
                lse = top[prows:] + jnp.log(total[prows:])
                stat = jnp.where(lanes == i, lse, stat)
                part_out[c, :, i * HD : (i + 1) * HD] = mixed[prows:]
                outs[c, :, i * HD : (i + 1) * HD] = mixed[:prows]
                if i == early - 1:
                    neighbour(c, end)[0].start()
            stat_out[c] = stat
            for cp in neighbour(c, end)[1:]:
                cp.start()
            send_out(outs, so, c, o_send, o_recv, o_loc)
        for c in range(nch):
            kv_copy(p, c, across, own_send.at[0, c]).wait_send()
            kv_copy(end, c, across, fwd_send.at[0, c]).wait_send()
            for cp in neighbour(c, end):
                cp.wait_send()

    if n_patch == 4:
        pl.when(is_end)(end_program)
        pl.when(jnp.logical_not(is_end))(helper_program)
    else:
        line_program()

    for a in range(4):
        for k in range(1, n_head):
            x_copy(a, k).wait_send()
    for src_ref, dst, send, recv, loc in (
        (outc, co, c_send, c_recv, c_loc),
        (outs, so, o_send, o_recv, o_loc),
    ):
        for c in range(nch):
            for k in range(1, n_head):
                cp = out_copy(src_ref, dst, c, k, send, recv)
                cp.wait_send()
                cp.wait_recv()
            local_out(src_ref, dst, c, loc).wait()


def store_kernel(a, b, so, co, sem):
    copies = [
        pltpu.make_async_copy(a, so, sem.at[0]),
        pltpu.make_async_copy(b, co, sem.at[1]),
    ]
    for cp in copies:
        cp.start()
    for cp in copies:
        cp.wait()


def store(a, b):
    return pl.pallas_call(
        store_kernel,
        out_shape=(
            jax.ShapeDtypeStruct(a.shape, a.dtype),
            jax.ShapeDtypeStruct(b.shape, b.dtype),
        ),
        in_specs=[pl.BlockSpec(memory_space=pltpu.VMEM)] * 2,
        out_specs=(pl.BlockSpec(memory_space=pltpu.HBM),) * 2,
        scratch_shapes=[pltpu.SemaphoreType.DMA((2,))],
        compiler_params=pltpu.CompilerParams(vmem_limit_bytes=1024 * 1024),
        name="store_outputs",
    )(a, b)


def per_device(n_patch, n_head, *args):
    fq, fk, fv, sk, sv, cq, tk, tv, mask = args
    rows = fq.shape[1]
    prows = rows * n_head
    hcols = sk.shape[2]
    heads = hcols // HD
    nch = 2 if heads % 2 == 0 else 1
    ccols = hcols // nch
    txt = tk.shape[1]
    peers = max(n_head - 1, 1)
    any_spec = pl.BlockSpec(memory_space=pl.ANY)
    dma = pltpu.SemaphoreType.DMA
    bf16 = jnp.bfloat16
    mixed = pl.pallas_call(
        functools.partial(kernel, n_patch, n_head, nch),
        out_shape=(
            pltpu.VMEM(fq.shape, bf16),
            pltpu.VMEM(cq.shape, bf16),
        ),
        in_specs=[any_spec] * 9,
        out_specs=(pl.BlockSpec(memory_space=pltpu.VMEM),) * 2,
        scratch_shapes=[
            pltpu.VMEM((4, prows, hcols), bf16),
            pltpu.VMEM((n_patch, nch, 2, prows, ccols), bf16),
            pltpu.VMEM((txt, hcols), bf16),
            pltpu.VMEM((txt, hcols), bf16),
            pltpu.VMEM((1, txt), jnp.int32),
            pltpu.VMEM((nch, prows, ccols), bf16),
            pltpu.VMEM((nch, prows, ccols), bf16),
            dma((4, peers)),
            dma((4, peers)),
            dma((4,)),
            dma((3,)),
            dma((nch, 2)),
            dma((2, nch)),
            dma((n_patch, nch)),
            dma((n_patch, nch)),
            dma((nch, peers)),
            dma((nch, peers)),
            dma((nch,)),
            dma((nch, peers)),
            dma((nch, peers)),
            dma((nch,)),
            pltpu.VMEM((prows, hcols), bf16),
            pltpu.VMEM((nch, prows, ccols), bf16),
            pltpu.VMEM((nch, prows, ccols), bf16),
            pltpu.VMEM((nch, prows, HD), jnp.float32),
            pltpu.VMEM((nch, prows, HD), jnp.float32),
            dma((2,)),
            dma((nch, 3)),
            dma((nch, 3)),
        ],
        compiler_params=pltpu.CompilerParams(collective_id=0, has_side_effects=True),
        name="displaced_attention",
    )(*args)
    return store(*mixed)


def solution(mesh):
    return jax.shard_map(
        functools.partial(per_device, mesh.shape["patch"], mesh.shape["head"]),
        mesh=mesh,
        in_specs=(
            P(("group", "cfg"), ("patch", "head"), None),
            P(("group", "cfg"), ("patch", "head"), None),
            P(("group", "cfg"), ("patch", "head"), None),
            P(("group", "cfg"), "patch", "head"),
            P(("group", "cfg"), "patch", "head"),
            P(("group", "cfg"), ("patch", "head"), None),
            P(("group", "cfg"), None, "head"),
            P(("group", "cfg"), None, "head"),
            P(("group", "cfg"), None),
        ),
        out_specs=(
            P(("group", "cfg"), ("patch", "head"), None),
            P(("group", "cfg"), ("patch", "head"), None),
        ),
        check_vma=False,
    )
```
